32 devices in a mesh: dp: 16 (over z, x, core), tensor: 2 (over y).
Axes of the slice: x: 2, y: 2, z: 4, core: 2. Of those that a mesh axis runs over, the one named last changes fastest.
Arguments:
- inputs: bfloat16 [640, 64, 1024], P('tensor', 'dp'), may hold values from -6 to 6
- pad_mask: int32 [64, 640], P('dp'), may hold values from 0 to 1, as said below
- norm1_gain: bfloat16 [2, 512], P('tensor', 'dp'), may hold values from 0.099609375 to 1.8984375
- norm1_shift: bfloat16 [2, 512], P('tensor', 'dp'), may hold values from -3 to 3
- qkv_weight: bfloat16 [1024, 3, 1024], P('dp', None, 'tensor'), may hold values from -0.1875 to 0.1875
- qv_bias: bfloat16 [2, 2, 512], P(None, 'tensor', 'dp'), may hold values from -3 to 3
- out_weight: bfloat16 [1024, 1024], P('tensor', 'dp'), may hold values from -3 to 3
- out_bias: bfloat16 [2, 512], P('tensor', 'dp'), may hold values from -3 to 3
- norm2_gain: bfloat16 [2, 512], P('tensor', 'dp'), may hold values from 0.099609375 to 1.8984375
- norm2_shift: bfloat16 [2, 512], P('tensor', 'dp'), may hold values from -3 to 3
- up_weight: bfloat16 [1024, 4096], P('dp', 'tensor'), may hold values from -0.1875 to 0.1875
- up_bias: bfloat16 [2, 2048], P('tensor', 'dp'), may hold values from -3 to 3
- down_weight: bfloat16 [4096, 1024], P('tensor', 'dp'), may hold values from -0.09375 to 0.09375
- down_bias: bfloat16 [2, 512], P('tensor', 'dp'), may hold values from -3 to 3
- cotangent: float32 [640, 64, 1024], P('tensor', 'dp'), may hold values from -6 to 6
Outputs:
- block_output: float32 [640, 64, 1024], P('tensor', 'dp')
- input_grad: float32 [640, 64, 1024], P('tensor', 'dp')
- gain_one_grad: float32 [2, 512], P('tensor', 'dp')
- shift_one_grad: float32 [2, 512], P('tensor', 'dp')
- qkv_weight_grad: float32 [1024, 3, 1024], P('dp', None, 'tensor')
- qv_bias_grad: float32 [2, 2, 512], P(None, 'tensor', 'dp')
- out_weight_grad: float32 [1024, 1024], P('tensor', 'dp')
- out_bias_grad: float32 [2, 512], P('tensor', 'dp')
- gain_two_grad: float32 [2, 512], P('tensor', 'dp')
- shift_two_grad: float32 [2, 512], P('tensor', 'dp')
- up_weight_grad: float32 [1024, 4096], P('dp', 'tensor')
- up_bias_grad: float32 [2, 2048], P('tensor', 'dp')
- down_weight_grad: float32 [4096, 1024], P('tensor', 'dp')
- down_bias_grad: float32 [2, 512], P('tensor', 'dp')
The draws below stay inside these ranges and needn't reach their ends.
Inputs may be any that keep to these rules, and one draw needn't show every extreme that they name: `pad_mask`: each image's row holds ones on its first slots and zeros after them; it has between 289 and 577 ones, and image 0 has exactly 577.
All inputs are finite; a program needn't handle non-finite values.
Results may differ from the reference program's by a relative error of at most 0.0085.
The reference program's roundings to bfloat16 on the way count: a program that leaves them out, or rounds other values in their place, can miss the bound.
Values may be sent and summed in bfloat16 or wider, within the bound.
No kernel may reach another device: no remote copies, remote signals or barrier semaphores. Data moves between devices by JAX's collectives and lax.ppermute only.
A program may use at most 256 MiB of HBM per device.

```python
import jax
import jax.numpy as jnp
from jax import lax

D = 1024
HEADS = 16
HD = 64
FF = 4096
SEQ = 640
VALID = 577
IMAGES = 64
N_TENSOR = 2


def draw_pad_mask(key, part):
    lengths = jax.random.randint(key, (IMAGES,), VALID // 2 + 1, VALID + 1)
    lengths = jnp.where(jnp.arange(IMAGES) == 0, VALID, lengths)
    positions = jnp.arange(SEQ)
    return (positions[None, :] < lengths[:, None]).astype(jnp.int32)


def block_levels(own_key, shape, cuts, smallest, top_value):
    level, own = 1.0, jax.random.fold_in(own_key, 6)
    for dim, shards_of in cuts:
        draws = jnp.exp(jax.random.uniform(jax.random.fold_in(own, dim), (shards_of,), jnp.float32, smallest / len(cuts), top_value / len(cuts)))
        level = level * jnp.repeat(draws, shape[dim] // shards_of).reshape([-1 if axis == dim else 1 for axis in range(len(shape))])
    return level


def bell_draw(stream_key, shape, deviation, most, cuts=(), held_as=jnp.bfloat16):
    drawn = deviation * jax.random.normal(stream_key, shape, jnp.float32)
    if cuts:
        drawn = drawn * block_levels(stream_key, shape, cuts, -0.22, 0.18)
    return jnp.clip(drawn, -most, most).astype(held_as)


def setup_inputs(seed: int = 0) -> dict:
    key_of = jax.random.split(jax.random.key(seed), 16)
    return {
        "inputs": bell_draw(key_of[0], (SEQ, IMAGES, D), 1.0, 6.0, ((0, 2), (1, 16))),
        "pad_mask": draw_pad_mask(jax.random.fold_in(key_of[15], 71), 0),
        "norm1_gain": jnp.clip(1.0 + 0.18 * jax.random.normal(key_of[2], (N_TENSOR, D // N_TENSOR), jnp.float32), 0.099609375, 1.8984375).astype(jnp.bfloat16),
        "norm1_shift": bell_draw(key_of[3], (N_TENSOR, D // N_TENSOR), 0.5, 3.0, ((0, 2), (1, 16))),
        "qkv_weight": bell_draw(key_of[4], (D, 3, D), D ** -0.5, 0.1875, ((0, 16), (2, 2))),
        "qv_bias": bell_draw(key_of[5], (2, N_TENSOR, D // N_TENSOR), 0.5, 3.0, ((1, 2), (2, 16))),
        "out_weight": bell_draw(key_of[6], (D, D), (D // 256) ** -0.5, 3.0, ((0, 2), (1, 16))),
        "out_bias": bell_draw(key_of[7], (N_TENSOR, D // N_TENSOR), 0.5, 3.0, ((0, 2), (1, 16))),
        "norm2_gain": jnp.clip(1.0 + 0.18 * jax.random.normal(key_of[8], (N_TENSOR, D // N_TENSOR), jnp.float32), 0.099609375, 1.8984375).astype(jnp.bfloat16),
        "norm2_shift": bell_draw(key_of[9], (N_TENSOR, D // N_TENSOR), 0.5, 3.0, ((0, 2), (1, 16))),
        "up_weight": bell_draw(key_of[10], (D, FF), D ** -0.5, 0.1875, ((0, 16), (1, 2))),
        "up_bias": bell_draw(key_of[11], (N_TENSOR, FF // N_TENSOR), 0.5, 3.0, ((0, 2), (1, 16))),
        "down_weight": bell_draw(key_of[12], (FF, D), FF ** -0.5, 0.09375, ((0, 2), (1, 16))),
        "down_bias": bell_draw(key_of[13], (N_TENSOR, D // N_TENSOR), 0.5, 3.0, ((0, 2), (1, 16))),
        "cotangent": bell_draw(key_of[14], (SEQ, IMAGES, D), 1.0, 6.0, ((0, 2), (1, 16)), jnp.float32),
    }


@jax.custom_vjp
def low(v):
    return lax.optimization_barrier(v.astype(jnp.bfloat16)).astype(jnp.float32)

@jax.custom_vjp
def low_back(v):
    return v

def low_keep(v):
    return (low(v), None)

def low_pass(kept, grad):
    return (grad,)

def back_keep(v):
    return (v, None)

def back_low(kept, grad):
    return (low(grad),)
low.defvjp(low_keep, low_pass)
low_back.defvjp(back_keep, back_low)
epsilon = 1e-06
masked_score = -1e+30
highest = lax.Precision.HIGHEST

def layer_norm(values, gain, shift):
    row_mean = lax.optimization_barrier(jnp.mean(values, axis=-1, keepdims=True))
    centred = values - row_mean
    spread = lax.optimization_barrier(jnp.mean(centred * centred, axis=-1, keepdims=True))
    return centred * lax.rsqrt(spread + epsilon) * gain + shift

def block_forward(params, inputs_group, mask_group):
    gain_one, shift_one, qkv_matrix, qv_shift, out_matrix, out_shift, gain_two, shift_two, up_matrix, up_shift, down_matrix, down_shift = params
    group_size, seq_length, model_width = inputs_group.shape
    kept = mask_group > 0
    normed_one = low(layer_norm(inputs_group, gain_one, shift_one))
    qkv_shift = jnp.concatenate([qv_shift[0], jnp.zeros((model_width,), jnp.float32), qv_shift[1]])
    qkv_rows = jnp.dot(normed_one, qkv_matrix, precision=highest) + qkv_shift
    qkv_rows = low_back(low(qkv_rows)).reshape(group_size, seq_length, 3, HEADS, HD)
    queries = qkv_rows[:, :, 0]
    key_rows = qkv_rows[:, :, 1]
    value_rows = qkv_rows[:, :, 2]
    scores = jnp.einsum('gqhe,gkhe->ghqk', queries, key_rows, precision=highest) * HD ** (-0.5)
    scores = low_back(scores)
    scores = jnp.where(kept[:, None, None, :], scores, masked_score)
    soft_weights = low(jax.nn.softmax(scores, axis=-1))
    attended = jnp.einsum('ghqk,gkhe->gqhe', soft_weights, value_rows, precision=highest)
    attended = low_back(low(attended)).reshape(group_size, seq_length, model_width)
    projected = low_back(jnp.dot(attended, out_matrix, precision=highest))
    after_attn = inputs_group + projected + out_shift
    normed_two = low(layer_norm(after_attn, gain_two, shift_two))
    up_values = low_back(jnp.dot(normed_two, up_matrix, precision=highest) + up_shift)
    activated = low(jax.nn.gelu(up_values, approximate=False))
    mlp_out = low_back(jnp.dot(activated, down_matrix, precision=highest))
    return (after_attn + mlp_out + down_shift) * kept[..., None].astype(jnp.float32)

def to_float(array, shape):
    return array.astype(jnp.float32).reshape(shape)

def reference(inputs, pad_mask, norm1_gain, norm1_shift, qkv_weight, qv_bias, out_weight, out_bias, norm2_gain, norm2_shift, up_weight, up_bias, down_weight, down_bias, cotangent):
    seq_length, image_count, model_width = inputs.shape
    hidden_width = up_weight.shape[1]
    groups = image_count // 4
    params = (to_float(norm1_gain, (model_width,)), to_float(norm1_shift, (model_width,)), to_float(qkv_weight, (model_width, 3 * model_width)), to_float(qv_bias, (2, model_width)), to_float(out_weight, (model_width, model_width)), to_float(out_bias, (model_width,)), to_float(norm2_gain, (model_width,)), to_float(norm2_shift, (model_width,)), to_float(up_weight, (model_width, hidden_width)), to_float(up_bias, (hidden_width,)), to_float(down_weight, (hidden_width, model_width)), to_float(down_bias, (model_width,)))
    inputs_all = jnp.transpose(inputs.astype(jnp.float32), (1, 0, 2)).reshape(groups, 4, seq_length, model_width)
    cotangent_all = jnp.transpose(cotangent.astype(jnp.float32), (1, 0, 2)).reshape(groups, 4, seq_length, model_width)
    masks = pad_mask.reshape(groups, 4, seq_length)
    checked = jax.checkpoint(block_forward)

    def forward_all(params_in, inputs_in):

        def scan_step(carried, operands):
            return (carried, checked(params_in, operands[0], operands[1]))
        return lax.scan(scan_step, jnp.zeros((), jnp.float32), (inputs_in, masks))[1]
    outputs, pullback = jax.vjp(forward_all, params, inputs_all)
    param_grads, input_grads = pullback(cotangent_all)

    def to_layout(array):
        return jnp.transpose(array.reshape(image_count, seq_length, model_width), (1, 0, 2))
    vector_shape = (N_TENSOR, model_width // N_TENSOR)
    return (to_layout(outputs), to_layout(input_grads), param_grads[0].reshape(vector_shape), param_grads[1].reshape(vector_shape), param_grads[2].reshape(model_width, 3, model_width), param_grads[3].reshape(2, N_TENSOR, model_width // N_TENSOR), param_grads[4], param_grads[5].reshape(vector_shape), param_grads[6].reshape(vector_shape), param_grads[7].reshape(vector_shape), param_grads[8], param_grads[9].reshape(N_TENSOR, hidden_width // N_TENSOR), param_grads[10], param_grads[11].reshape(vector_shape))
```

```python
import functools

import jax
import jax.numpy as jnp
from jax import lax
from jax.experimental import pallas as pl
from jax.experimental.pallas import tpu as pltpu
from jax.sharding import PartitionSpec as P

HD = 64
PAIR = 2 * HD
VALID = 577
F32 = jnp.float32
BF16 = jnp.bfloat16

epsilon = 1e-06
masked_score = -1e30


def layer_norm(values, gain, shift):
    row_mean = jnp.mean(values, axis=-1, keepdims=True)
    centred = values - row_mean
    spread = jnp.mean(centred * centred, axis=-1, keepdims=True)
    return centred * lax.rsqrt(spread + epsilon) * gain + shift


def gelu_exact(values):
    return jax.nn.gelu(values, approximate=False)


def image_scores(queries, key_rows, kept_row):
    scores = jnp.einsum(
        "qhe,khe->hqk", queries, key_rows, preferred_element_type=jnp.float32
    ) * HD ** (-0.5)
    return jnp.where(kept_row[None, None, :], scores, masked_score)


def forward_image(operands):
    queries, key_rows, value_rows, kept_row = operands
    scores = image_scores(queries, key_rows, kept_row)
    row_max = jnp.max(scores, axis=-1, keepdims=True)
    exps = jnp.exp(scores - row_max)
    row_total = jnp.sum(exps, axis=-1, keepdims=True)
    soft_weights = (exps / row_total).astype(jnp.bfloat16)
    attended = jnp.einsum(
        "hqk,khe->qhe", soft_weights, value_rows, preferred_element_type=jnp.float32
    )
    return (attended.astype(jnp.bfloat16), (row_max + jnp.log(row_total))[..., 0])


def backward_image(operands):
    queries, key_rows, value_rows, kept_row, log_total, attended_grad = operands
    seq_length = queries.shape[0]
    scores = image_scores(queries, key_rows, kept_row)
    soft_float = jnp.exp(scores - log_total[..., None])
    soft_weights = soft_float.astype(jnp.bfloat16)
    value_grad = jnp.einsum(
        "hqk,qhe->khe", soft_weights, attended_grad, preferred_element_type=jnp.float32
    )
    prob_grad = jnp.einsum(
        "qhe,khe->hqk", attended_grad, value_rows, preferred_element_type=jnp.float32
    )
    score_grad = soft_float * (prob_grad - jnp.sum(prob_grad * soft_float, axis=-1, keepdims=True))
    score_grad = score_grad.astype(jnp.bfloat16)
    query_grad = jnp.einsum(
        "hqk,khe->qhe", score_grad, key_rows, preferred_element_type=jnp.float32
    ) * HD ** (-0.5)
    key_grad = jnp.einsum(
        "hqk,qhe->khe", score_grad, queries, preferred_element_type=jnp.float32
    ) * HD ** (-0.5)
    joined = jnp.concatenate(
        [
            query_grad.reshape(seq_length, -1),
            key_grad.reshape(seq_length, -1),
            value_grad.reshape(seq_length, -1),
        ],
        axis=-1,
    )
    return joined.astype(jnp.bfloat16)


def on_device(
    inputs,
    pad_mask,
    norm1_gain,
    norm1_shift,
    qkv_weight,
    qv_bias,
    out_weight,
    out_bias,
    norm2_gain,
    norm2_shift,
    up_weight,
    up_bias,
    down_weight,
    down_bias,
    cotangent,
):
    local_rows = inputs.shape[0]
    image_count = inputs.shape[1]
    model_width = inputs.shape[2]
    seq_length = pad_mask.shape[1]
    tensor_count = lax.axis_size("tensor")
    vector_stack = jnp.stack(
        [norm1_gain, norm1_shift, out_bias, norm2_gain, norm2_shift, down_bias], axis=0
    )
    gathered = (
        lax.all_gather(qkv_weight, "dp", axis=0, tiled=True),
        lax.all_gather(out_weight, "dp", axis=1, tiled=True),
        lax.all_gather(up_weight, "dp", axis=0, tiled=True),
        lax.all_gather(down_weight, "dp", axis=1, tiled=True),
        lax.all_gather(qv_bias, "dp", axis=2, tiled=True),
        lax.all_gather(up_bias, "dp", axis=1, tiled=True),
        lax.all_gather(vector_stack, "dp", axis=2, tiled=True),
    )
    qkv_full, out_full, up_full, down_full, bias_pair, bias_hidden, vector_part = gathered
    local_width = qkv_full.shape[2]
    head_count = local_width // HD
    vector_rows = (
        lax.all_gather(vector_part, "tensor", axis=1, tiled=True)
        .reshape(6, model_width)
        .astype(jnp.float32)
    )
    gain_one, shift_one, out_shift, gain_two, shift_two, down_shift = [
        vector_rows[index] for index in range(6)
    ]
    qkv_matrix = qkv_full.reshape(model_width, 3 * local_width)
    bias_row = jnp.concatenate(
        [
            bias_pair[0, 0].astype(jnp.float32),
            jnp.zeros((local_width,), jnp.float32),
            bias_pair[1, 0].astype(jnp.float32),
        ]
    )
    up_row = bias_hidden.reshape(-1).astype(jnp.float32)
    kept_all = pad_mask > 0
    first_row = lax.axis_index("tensor") * local_rows
    kept_float = jnp.transpose(lax.dynamic_slice_in_dim(kept_all, first_row, local_rows, 1)).astype(
        jnp.float32
    )[:, :, None]
    input_float = inputs.astype(jnp.float32)
    normed_one = layer_norm(input_float, gain_one, shift_one).astype(jnp.bfloat16)
    normed_all = lax.all_gather(normed_one, "tensor", axis=0, tiled=True)
    qkv_rows = (
        jnp.einsum("sbd,dc->sbc", normed_all, qkv_matrix, preferred_element_type=jnp.float32)
        + bias_row
    )
    qkv_rows = qkv_rows.astype(jnp.bfloat16)
    qkv_images = jnp.swapaxes(qkv_rows, 0, 1).reshape(image_count, seq_length, 3, head_count, HD)
    query_all = qkv_images[:, :, 0]
    key_all = qkv_images[:, :, 1]
    value_all = qkv_images[:, :, 2]
    attended_img, log_totals = lax.map(forward_image, (query_all, key_all, value_all, kept_all))
    attended_rows = jnp.swapaxes(attended_img.reshape(image_count, seq_length, local_width), 0, 1)
    row_block = attended_rows
    projected = lax.psum_scatter(
        jnp.einsum("sbc,cd->sbd", row_block, out_full, preferred_element_type=jnp.float32),
        "tensor",
        scatter_dimension=0,
        tiled=True,
    )
    after_attn = input_float + projected + out_shift
    normed_two = layer_norm(after_attn, gain_two, shift_two).astype(jnp.bfloat16)
    normed_all_two = lax.all_gather(normed_two, "tensor", axis=0, tiled=True)
    up_values = (
        jnp.einsum("sbd,df->sbf", normed_all_two, up_full, preferred_element_type=jnp.float32)
        + up_row
    )
    activated = gelu_exact(up_values).astype(jnp.bfloat16)
    row_block = activated
    mlp_out = lax.psum_scatter(
        jnp.einsum("sbf,fd->sbd", row_block, down_full, preferred_element_type=jnp.float32),
        "tensor",
        scatter_dimension=0,
        tiled=True,
    )
    block_output = (after_attn + mlp_out + down_shift) * kept_float
    qkv_back, out_back, up_back, down_back = (qkv_matrix, out_full, up_full, down_full)
    out_grad = cotangent * kept_float
    down_shift_grad = jnp.sum(out_grad, axis=(0, 1))
    out_low = out_grad.astype(jnp.bfloat16)
    out_low_all = lax.all_gather(out_low, "tensor", axis=0, tiled=True)
    down_weight_grad = jnp.einsum(
        "sbf,sbd->fd", activated, out_low_all, preferred_element_type=jnp.float32
    )
    act_grad = jnp.einsum("sbd,fd->sbf", out_low_all, down_back, preferred_element_type=jnp.float32)
    _, gelu_back = jax.vjp(gelu_exact, up_values)
    up_grad = gelu_back(act_grad)[0].astype(jnp.bfloat16)
    up_shift_grad = jnp.sum(up_grad.astype(jnp.float32), axis=(0, 1))
    up_weight_grad = jnp.einsum(
        "sbd,sbf->df", normed_all_two, up_grad, preferred_element_type=jnp.float32
    )
    row_block = up_grad
    normed_two_grad = lax.psum_scatter(
        jnp.einsum("sbf,df->sbd", row_block, up_back, preferred_element_type=jnp.float32),
        "tensor",
        scatter_dimension=0,
        tiled=True,
    )
    _, norm_two_back = jax.vjp(layer_norm, after_attn, gain_two, shift_two)
    attn_side, gain_two_grad, shift_two_grad = norm_two_back(normed_two_grad)
    after_attn_grad = out_grad + attn_side
    out_shift_grad = jnp.sum(after_attn_grad, axis=(0, 1))
    proj_low = after_attn_grad.astype(jnp.bfloat16)
    proj_low_all = lax.all_gather(proj_low, "tensor", axis=0, tiled=True)
    out_weight_grad = jnp.einsum(
        "sbc,sbd->cd", attended_rows, proj_low_all, preferred_element_type=jnp.float32
    )
    attended_grad = jnp.einsum(
        "sbd,cd->sbc", proj_low_all, out_back, preferred_element_type=jnp.float32
    )
    attended_grad = attended_grad.astype(jnp.bfloat16)
    attended_grad_img = jnp.swapaxes(attended_grad, 0, 1).reshape(
        image_count, seq_length, head_count, HD
    )
    qkv_grad_img = lax.map(
        backward_image, (query_all, key_all, value_all, kept_all, log_totals, attended_grad_img)
    )
    qkv_grad = jnp.swapaxes(qkv_grad_img, 0, 1)
    qkv_sums = jnp.sum(qkv_grad.astype(jnp.float32), axis=(0, 1))
    qv_grad = jnp.stack([qkv_sums[:local_width], qkv_sums[2 * local_width :]], axis=0).reshape(
        2, 1, local_width
    )
    qkv_weight_grad = jnp.einsum(
        "sbd,sbc->dc", normed_all, qkv_grad, preferred_element_type=jnp.float32
    )
    qkv_weight_grad = qkv_weight_grad.reshape(model_width, 3, local_width)
    row_block = qkv_grad
    normed_one_grad = lax.psum_scatter(
        jnp.einsum("sbc,dc->sbd", row_block, qkv_back, preferred_element_type=jnp.float32),
        "tensor",
        scatter_dimension=0,
        tiled=True,
    )
    _, norm_one_back = jax.vjp(layer_norm, input_float, gain_one, shift_one)
    input_side, gain_one_grad, shift_one_grad = norm_one_back(normed_one_grad)
    input_grad = after_attn_grad + input_side
    vector_grads = jnp.stack(
        [
            gain_one_grad,
            shift_one_grad,
            out_shift_grad,
            gain_two_grad,
            shift_two_grad,
            down_shift_grad,
        ],
        axis=0,
    ).reshape(6, tensor_count, model_width // tensor_count)
    vector_local = lax.psum_scatter(vector_grads, "tensor", scatter_dimension=1, tiled=True)
    owned = (
        lax.psum_scatter(qkv_weight_grad, "dp", scatter_dimension=0, tiled=True),
        lax.psum_scatter(out_weight_grad, "dp", scatter_dimension=1, tiled=True),
        lax.psum_scatter(up_weight_grad, "dp", scatter_dimension=0, tiled=True),
        lax.psum_scatter(down_weight_grad, "dp", scatter_dimension=1, tiled=True),
        lax.psum_scatter(qv_grad, "dp", scatter_dimension=2, tiled=True),
        lax.psum_scatter(up_shift_grad.reshape(1, -1), "dp", scatter_dimension=1, tiled=True),
        lax.psum_scatter(vector_local, "dp", scatter_dimension=2, tiled=True),
    )
    qkv_owned, out_owned, up_owned, down_owned, qv_owned, hidden_owned, vector_owned = owned
    return (
        block_output,
        input_grad,
        vector_owned[0],
        vector_owned[1],
        qkv_owned,
        qv_owned,
        out_owned,
        vector_owned[2],
        vector_owned[3],
        vector_owned[4],
        up_owned,
        hidden_owned,
        down_owned,
        vector_owned[5],
    )


BOTH = ("tensor", "dp")
NT = (((1,), (1,)), ((), ()))
NN = (((1,), (0,)), ((), ()))


def dot_nn(a, b):
    return lax.dot_general(a, b, NN, preferred_element_type=F32)


def dot_nt(a, b):
    return lax.dot_general(a, b, NT, preferred_element_type=F32)


def attention_forward_kernel(lengths, q_ref, k_ref, v_ref, o_ref, lse_ref, *, key_rows):
    length = lengths[pl.program_id(0)]
    queries = q_ref[0] * jnp.asarray(HD**-0.5, BF16)
    keys = k_ref[0, :key_rows]
    values_t = jnp.transpose(v_ref[0, :key_rows].astype(F32)).astype(BF16)
    lane = lax.broadcasted_iota(jnp.int32, (key_rows, PAIR), 1)
    valid = lax.broadcasted_iota(jnp.int32, (key_rows, q_ref.shape[1]), 0) < length
    outs = []
    for head in range(2):
        own = (lane >= head * HD) & (lane < (head + 1) * HD)
        scores = dot_nt(jnp.where(own, keys, jnp.zeros_like(keys)), queries)
        scores = jnp.where(valid, scores, masked_score)
        top = jnp.max(scores, axis=0, keepdims=True)
        exps = jnp.exp(scores - top)
        total = jnp.sum(exps, axis=0, keepdims=True)
        lse_ref[0, 0, head : head + 1, :] = top + jnp.log(total)
        probs = (exps * (1.0 / total)).astype(BF16)
        outs.append(dot_nn(values_t[head * HD : (head + 1) * HD], probs))
    o_ref[0] = jnp.transpose(jnp.concatenate(outs, axis=0)).astype(BF16)


def attention_backward_kernel(
    lengths, q_ref, k_ref, v_ref, lse_ref, g_ref, dq_ref, dk_ref, dv_ref, *, key_rows
):
    length = lengths[pl.program_id(0)]
    slots = q_ref.shape[1]
    scale = HD**-0.5
    plain = q_ref[0]
    queries = plain * jnp.asarray(scale, BF16)
    keys = k_ref[0, :key_rows]
    values = v_ref[0, :key_rows]
    grads = g_ref[0]
    keys_t = jnp.transpose(keys.astype(F32)).astype(BF16)
    lane = lax.broadcasted_iota(jnp.int32, (key_rows, PAIR), 1)
    valid = lax.broadcasted_iota(jnp.int32, (key_rows, slots), 0) < length
    zero = jnp.zeros_like(keys)
    dqs, dks, dvs = [], [], []
    for head in range(2):
        own = (lane >= head * HD) & (lane < (head + 1) * HD)
        scores = dot_nt(jnp.where(own, keys, zero), queries)
        soft = jnp.where(valid, jnp.exp(scores - lse_ref[0, 0, head : head + 1, :]), 0.0)
        prob_grad = dot_nt(jnp.where(own, values, zero), grads)
        inner = jnp.sum(prob_grad * soft, axis=0, keepdims=True)
        score_grad = (soft * (prob_grad - inner)).astype(BF16)
        dvs.append(dot_nn(soft.astype(BF16), grads))
        dks.append(dot_nn(score_grad, plain))
        dqs.append(dot_nn(keys_t[head * HD : (head + 1) * HD], score_grad))
    first = lane < HD
    dq_ref[0] = (jnp.transpose(jnp.concatenate(dqs, axis=0)) * scale).astype(BF16)
    dk_ref[0, :key_rows] = (jnp.where(first, dks[0], dks[1]) * scale).astype(BF16)
    dv_ref[0, :key_rows] = jnp.where(first, dvs[0], dvs[1]).astype(BF16)
    if key_rows < slots:
        rest = jnp.zeros((slots - key_rows, PAIR), BF16)
        dk_ref[0, key_rows:] = rest
        dv_ref[0, key_rows:] = rest


def key_count(slots):
    return min(slots, -(-VALID // 16) * 16)


def attention_forward(lengths, qkv):
    images, slots, columns = qkv.shape
    width = columns // 3
    pairs = width // PAIR
    part = lambda offset: pl.BlockSpec((1, slots, PAIR), lambda b, p, ln: (b, 0, offset + p))
    return pl.pallas_call(
        functools.partial(attention_forward_kernel, key_rows=key_count(slots)),
        out_shape=(
            jax.ShapeDtypeStruct((images, slots, width), BF16),
            jax.ShapeDtypeStruct((images, pairs, 2, slots), F32),
        ),
        grid_spec=pltpu.PrefetchScalarGridSpec(
            num_scalar_prefetch=1,
            grid=(images, pairs),
            in_specs=[part(0), part(pairs), part(2 * pairs)],
            out_specs=(
                part(0),
                pl.BlockSpec((1, 1, 2, slots), lambda b, p, ln: (b, p, 0, 0)),
            ),
        ),
        compiler_params=pltpu.CompilerParams(vmem_limit_bytes=48 << 20),
        cost_estimate=pl.CostEstimate(
            flops=images * pairs * 2 * 4 * slots * slots * PAIR,
            bytes_accessed=images * slots * width * 8,
            transcendentals=images * pairs * 2 * slots * slots,
        ),
        name="attention_forward",
    )(lengths, qkv, qkv, qkv)


def attention_backward(lengths, qkv, lse, grads):
    images, slots, columns = qkv.shape
    width = columns // 3
    pairs = width // PAIR
    part = lambda offset: pl.BlockSpec((1, slots, PAIR), lambda b, p, ln: (b, 0, offset + p))
    piece = jax.ShapeDtypeStruct((images, slots, width), BF16)
    return pl.pallas_call(
        functools.partial(attention_backward_kernel, key_rows=key_count(slots)),
        out_shape=(piece, piece, piece),
        grid_spec=pltpu.PrefetchScalarGridSpec(
            num_scalar_prefetch=1,
            grid=(images, pairs),
            in_specs=[
                part(0),
                part(pairs),
                part(2 * pairs),
                pl.BlockSpec((1, 1, 2, slots), lambda b, p, ln: (b, p, 0, 0)),
                part(0),
            ],
            out_specs=(part(0), part(0), part(0)),
        ),
        compiler_params=pltpu.CompilerParams(vmem_limit_bytes=48 << 20),
        cost_estimate=pl.CostEstimate(
            flops=images * pairs * 2 * 10 * slots * slots * PAIR,
            bytes_accessed=images * slots * width * 14,
            transcendentals=images * pairs * 2 * slots * slots,
        ),
        name="attention_backward",
    )(lengths, qkv, qkv, qkv, lse, grads)


def to_images(rows):
    count = lax.axis_size("tensor")
    if count == 1:
        return rows
    if count > 2:
        return lax.all_to_all(rows, "tensor", 0, 1, tiled=True)
    me = lax.axis_index("tensor")
    own, part = rows.shape[0] // 2, rows.shape[1]
    kept = lax.dynamic_slice_in_dim(rows, me * own, own, 0)
    sent = lax.dynamic_slice_in_dim(rows, (1 - me) * own, own, 0)
    came = lax.ppermute(sent, "tensor", [(0, 1), (1, 0)])
    whole = jnp.zeros((own, 2 * part) + rows.shape[2:], rows.dtype)
    whole = lax.dynamic_update_slice_in_dim(whole, kept, me * part, 1)
    return lax.dynamic_update_slice_in_dim(whole, came, (1 - me) * part, 1)


def to_slots(rows):
    count = lax.axis_size("tensor")
    if count == 1:
        return jnp.swapaxes(rows, 0, 1)
    if count > 2:
        return jnp.swapaxes(lax.all_to_all(rows, "tensor", 1, 0, tiled=True), 0, 1)
    me = lax.axis_index("tensor")
    own, part = rows.shape[0], rows.shape[1] // 2
    kept = lax.dynamic_slice_in_dim(rows, me * part, part, 1)
    sent = lax.dynamic_slice_in_dim(rows, (1 - me) * part, part, 1)
    came = lax.ppermute(sent, "tensor", [(0, 1), (1, 0)])
    first = jnp.where(me == 0, kept, came)
    second = jnp.where(me == 0, came, kept)
    return jnp.swapaxes(jnp.concatenate([first, second], axis=0), 0, 1)


def normalize(values):
    row_mean = jnp.mean(values, axis=-1, keepdims=True)
    centred = values - row_mean
    spread = jnp.mean(centred * centred, axis=-1, keepdims=True)
    inverse = lax.rsqrt(spread + epsilon)
    return centred * inverse, inverse


def normalize_back(grad, unit, inverse, gain):
    scaled = grad * gain
    mean_one = jnp.mean(scaled, axis=-1, keepdims=True)
    mean_two = jnp.mean(scaled * unit, axis=-1, keepdims=True)
    return inverse * (scaled - mean_one - unit * mean_two)


def gelu_pair(values):
    area = 0.5 * (1.0 + lax.erf(values * (0.5**0.5)))
    density = jnp.exp(-0.5 * values * values) * ((2.0 * jnp.pi) ** -0.5)
    return (values * area).astype(BF16), area + values * density


def token_sum(values):
    return jnp.sum(values.astype(F32), axis=(0, 1))


def by_images(
    inputs,
    pad_mask,
    norm1_gain,
    norm1_shift,
    qkv_weight,
    qv_bias,
    out_weight,
    out_bias,
    norm2_gain,
    norm2_shift,
    up_weight,
    up_bias,
    down_weight,
    down_bias,
    cotangent,
):
    width = inputs.shape[2]
    slots = pad_mask.shape[1]
    tensors = lax.axis_size("tensor")
    shards = lax.axis_size("dp") * tensors
    me = lax.axis_index("tensor")
    images = inputs.shape[1] // tensors
    head_width = qkv_weight.shape[2]
    hidden = up_weight.shape[1]
    piece = norm1_gain.shape[1]
    hidden_piece = up_bias.shape[1]

    flat = jnp.concatenate(
        [
            v.reshape(-1)
            for v in (norm1_gain, norm1_shift, out_bias, norm2_gain, norm2_shift, down_bias, qv_bias, up_bias)
        ]
    ).reshape(1, -1)
    flat = lax.all_gather(flat, BOTH, axis=0, tiled=True).astype(F32)
    gain_one, shift_one, out_shift, gain_two, shift_two, down_shift = [
        flat[:, n * piece : (n + 1) * piece].reshape(width) for n in range(6)
    ]
    query_bias = flat[:, 6 * piece : 7 * piece].reshape(tensors, head_width)
    value_bias = flat[:, 7 * piece : 8 * piece].reshape(tensors, head_width)
    up_row = flat[:, 8 * piece :].reshape(tensors, hidden)

    def gather(shard):
        whole = lax.all_gather(shard, BOTH, axis=0, tiled=True)
        return whole.reshape(tensors, -1, shard.shape[1])

    qkv_full = gather(qkv_weight.reshape(qkv_weight.shape[0], -1))
    out_full = gather(jnp.transpose(out_weight))
    up_full = gather(up_weight)
    down_full = gather(jnp.transpose(down_weight))

    mask = lax.dynamic_slice_in_dim(pad_mask, me * images, images, 0)
    lengths = jnp.sum(mask, axis=1).astype(jnp.int32)
    kept = (mask > 0).astype(F32)[:, :, None]
    x = to_images(jnp.swapaxes(inputs, 0, 1)).astype(F32)
    cot = to_images(jnp.swapaxes(cotangent, 0, 1))

    unit_one, inverse_one = normalize(x)
    normed_one = (unit_one * gain_one + shift_one).astype(BF16)
    parts = range(tensors)
    product = functools.partial(jnp.einsum, preferred_element_type=F32)
    qkvs, attendeds, lses = [], [], []
    for t in parts:
        bias = jnp.concatenate([query_bias[t], jnp.zeros((head_width,), F32), value_bias[t]])
        qkvs.append((product("bsd,dc->bsc", normed_one, qkv_full[t]) + bias).astype(BF16))
        attended, lse = attention_forward(lengths, qkvs[t])
        attendeds.append(attended)
        lses.append(lse)
    projected = sum(product("bsc,dc->bsd", attendeds[t], out_full[t]) for t in parts)
    after_attn = x + projected + out_shift
    unit_two, inverse_two = normalize(after_attn)
    normed_two = (unit_two * gain_two + shift_two).astype(BF16)
    acts, slopes = [], []
    for t in parts:
        up_values = product("bsd,df->bsf", normed_two, up_full[t]) + up_row[t]
        act, slope = gelu_pair(up_values)
        acts.append(act)
        slopes.append(slope)
    out_grad = cot * kept
    out_low = out_grad.astype(BF16)
    down_shift_grad = token_sum(out_grad)

    def scatter(grads):
        stacked = jnp.concatenate(grads, axis=0).astype(BF16)
        return lax.psum_scatter(stacked, BOTH, scatter_dimension=0, tiled=True).astype(F32)

    down_owned = scatter([product("bsd,bsf->df", out_low, acts[t]) for t in parts])
    up_grads = []
    for t in parts:
        act_grad = product("bsd,df->bsf", out_low, down_full[t])
        up_grads.append((act_grad * slopes[t]).astype(BF16))
    up_owned = scatter([product("bsd,bsf->df", normed_two, up_grads[t]) for t in parts])
    normed_two_grad = sum(product("bsf,df->bsd", up_grads[t], up_full[t]) for t in parts)
    mlp_out = sum(product("bsf,df->bsd", acts[t], down_full[t]) for t in parts)
    block_output = to_slots((after_attn + mlp_out + down_shift) * kept)
    up_shift_grad = jnp.stack([token_sum(up_grads[t]) for t in parts])
    gain_two_grad = token_sum(normed_two_grad * unit_two)
    shift_two_grad = token_sum(normed_two_grad)
    after_attn_grad = out_grad + normalize_back(normed_two_grad, unit_two, inverse_two, gain_two)
    out_shift_grad = token_sum(after_attn_grad)
    proj_low = after_attn_grad.astype(BF16)
    out_owned = scatter([product("bsd,bsc->dc", proj_low, attendeds[t]) for t in parts])
    pieces, query_sums, value_sums = [], [], []
    for t in parts:
        attended_grad = product("bsd,dc->bsc", proj_low, out_full[t]).astype(BF16)
        pieces.append(attention_backward(lengths, qkvs[t], lses[t], attended_grad))
        query_sums.append(token_sum(pieces[t][0]))
        value_sums.append(token_sum(pieces[t][2]))
    qkv_owned = scatter(
        [
            jnp.concatenate([product("bsd,bsc->dc", normed_one, p) for p in pieces[t]], axis=1)
            for t in parts
        ]
    )
    normed_one_grad = sum(
        product(
            "bsc,dc->bsd",
            pieces[t][n],
            qkv_full[t][:, n * head_width : (n + 1) * head_width],
        )
        for t in parts
        for n in range(3)
    )
    gain_one_grad = token_sum(normed_one_grad * unit_one)
    shift_one_grad = token_sum(normed_one_grad)
    input_grad = after_attn_grad + normalize_back(normed_one_grad, unit_one, inverse_one, gain_one)
    input_grad = to_slots(input_grad)

    vectors = [gain_one_grad, shift_one_grad, out_shift_grad, gain_two_grad, shift_two_grad, down_shift_grad]
    vectors += [jnp.stack(query_sums), jnp.stack(value_sums), up_shift_grad]
    small = jnp.concatenate([v.reshape(shards, -1) for v in vectors], axis=1)
    small = lax.psum_scatter(small, BOTH, scatter_dimension=0, tiled=True)
    row = lambda n: small[:, n * piece : (n + 1) * piece]
    return (
        block_output,
        input_grad,
        row(0),
        row(1),
        qkv_owned.reshape(qkv_weight.shape),
        jnp.stack([row(6), row(7)], axis=0),
        jnp.transpose(out_owned),
        row(2),
        row(3),
        row(4),
        up_owned,
        small[:, 8 * piece : 8 * piece + hidden_piece],
        jnp.transpose(down_owned),
        row(5),
    )


def solution(mesh):
    in_specs = (
        P("tensor", "dp", None),
        P("dp", None),
        P("tensor", "dp"),
        P("tensor", "dp"),
        P("dp", None, "tensor"),
        P(None, "tensor", "dp"),
        P("tensor", "dp"),
        P("tensor", "dp"),
        P("tensor", "dp"),
        P("tensor", "dp"),
        P("dp", "tensor"),
        P("tensor", "dp"),
        P("tensor", "dp"),
        P("tensor", "dp"),
        P("tensor", "dp", None),
    )
    out_specs = (
        P("tensor", "dp", None),
        P("tensor", "dp", None),
        P("tensor", "dp"),
        P("tensor", "dp"),
        P("dp", None, "tensor"),
        P(None, "tensor", "dp"),
        P("tensor", "dp"),
        P("tensor", "dp"),
        P("tensor", "dp"),
        P("tensor", "dp"),
        P("dp", "tensor"),
        P("tensor", "dp"),
        P("tensor", "dp"),
        P("tensor", "dp"),
    )
    dims = dict(zip(mesh.axis_names, mesh.devices.shape))

    def choose(inputs, *rest):
        whole_images = inputs.shape[1] % dims["tensor"] == 0
        return (by_images if whole_images else on_device)(inputs, *rest)

    return jax.shard_map(
        choose, mesh=mesh, in_specs=in_specs, out_specs=out_specs, check_vma=False
    )
```

```python
import functools

import jax
import jax.numpy as jnp
from jax import lax
from jax.experimental import pallas as pl
from jax.experimental.pallas import tpu as pltpu
from jax.sharding import PartitionSpec as P

HD = 64
PAIR = 2 * HD
VALID = 577
F32 = jnp.float32
BF16 = jnp.bfloat16

epsilon = 1e-06
masked_score = -1e30


def layer_norm(values, gain, shift):
    row_mean = jnp.mean(values, axis=-1, keepdims=True)
    centred = values - row_mean
    spread = jnp.mean(centred * centred, axis=-1, keepdims=True)
    return centred * lax.rsqrt(spread + epsilon) * gain + shift


def gelu_exact(values):
    return jax.nn.gelu(values, approximate=False)


def image_scores(queries, key_rows, kept_row):
    scores = jnp.einsum(
        "qhe,khe->hqk", queries, key_rows, preferred_element_type=jnp.float32
    ) * HD ** (-0.5)
    return jnp.where(kept_row[None, None, :], scores, masked_score)


def forward_image(operands):
    queries, key_rows, value_rows, kept_row = operands
    scores = image_scores(queries, key_rows, kept_row)
    row_max = jnp.max(scores, axis=-1, keepdims=True)
    exps = jnp.exp(scores - row_max)
    row_total = jnp.sum(exps, axis=-1, keepdims=True)
    soft_weights = (exps / row_total).astype(jnp.bfloat16)
    attended = jnp.einsum(
        "hqk,khe->qhe", soft_weights, value_rows, preferred_element_type=jnp.float32
    )
    return (attended.astype(jnp.bfloat16), (row_max + jnp.log(row_total))[..., 0])


def backward_image(operands):
    queries, key_rows, value_rows, kept_row, log_total, attended_grad = operands
    seq_length = queries.shape[0]
    scores = image_scores(queries, key_rows, kept_row)
    soft_float = jnp.exp(scores - log_total[..., None])
    soft_weights = soft_float.astype(jnp.bfloat16)
    value_grad = jnp.einsum(
        "hqk,qhe->khe", soft_weights, attended_grad, preferred_element_type=jnp.float32
    )
    prob_grad = jnp.einsum(
        "qhe,khe->hqk", attended_grad, value_rows, preferred_element_type=jnp.float32
    )
    score_grad = soft_float * (prob_grad - jnp.sum(prob_grad * soft_float, axis=-1, keepdims=True))
    score_grad = score_grad.astype(jnp.bfloat16)
    query_grad = jnp.einsum(
        "hqk,khe->qhe", score_grad, key_rows, preferred_element_type=jnp.float32
    ) * HD ** (-0.5)
    key_grad = jnp.einsum(
        "hqk,qhe->khe", score_grad, queries, preferred_element_type=jnp.float32
    ) * HD ** (-0.5)
    joined = jnp.concatenate(
        [
            query_grad.reshape(seq_length, -1),
            key_grad.reshape(seq_length, -1),
            value_grad.reshape(seq_length, -1),
        ],
        axis=-1,
    )
    return joined.astype(jnp.bfloat16)


def on_device(
    inputs,
    pad_mask,
    norm1_gain,
    norm1_shift,
    qkv_weight,
    qv_bias,
    out_weight,
    out_bias,
    norm2_gain,
    norm2_shift,
    up_weight,
    up_bias,
    down_weight,
    down_bias,
    cotangent,
):
    local_rows = inputs.shape[0]
    image_count = inputs.shape[1]
    model_width = inputs.shape[2]
    seq_length = pad_mask.shape[1]
    tensor_count = lax.axis_size("tensor")
    vector_stack = jnp.stack(
        [norm1_gain, norm1_shift, out_bias, norm2_gain, norm2_shift, down_bias], axis=0
    )
    gathered = (
        lax.all_gather(qkv_weight, "dp", axis=0, tiled=True),
        lax.all_gather(out_weight, "dp", axis=1, tiled=True),
        lax.all_gather(up_weight, "dp", axis=0, tiled=True),
        lax.all_gather(down_weight, "dp", axis=1, tiled=True),
        lax.all_gather(qv_bias, "dp", axis=2, tiled=True),
        lax.all_gather(up_bias, "dp", axis=1, tiled=True),
        lax.all_gather(vector_stack, "dp", axis=2, tiled=True),
    )
    qkv_full, out_full, up_full, down_full, bias_pair, bias_hidden, vector_part = gathered
    local_width = qkv_full.shape[2]
    head_count = local_width // HD
    vector_rows = (
        lax.all_gather(vector_part, "tensor", axis=1, tiled=True)
        .reshape(6, model_width)
        .astype(jnp.float32)
    )
    gain_one, shift_one, out_shift, gain_two, shift_two, down_shift = [
        vector_rows[index] for index in range(6)
    ]
    qkv_matrix = qkv_full.reshape(model_width, 3 * local_width)
    bias_row = jnp.concatenate(
        [
            bias_pair[0, 0].astype(jnp.float32),
            jnp.zeros((local_width,), jnp.float32),
            bias_pair[1, 0].astype(jnp.float32),
        ]
    )
    up_row = bias_hidden.reshape(-1).astype(jnp.float32)
    kept_all = pad_mask > 0
    first_row = lax.axis_index("tensor") * local_rows
    kept_float = jnp.transpose(lax.dynamic_slice_in_dim(kept_all, first_row, local_rows, 1)).astype(
        jnp.float32
    )[:, :, None]
    input_float = inputs.astype(jnp.float32)
    normed_one = layer_norm(input_float, gain_one, shift_one).astype(jnp.bfloat16)
    normed_all = lax.all_gather(normed_one, "tensor", axis=0, tiled=True)
    qkv_rows = (
        jnp.einsum("sbd,dc->sbc", normed_all, qkv_matrix, preferred_element_type=jnp.float32)
        + bias_row
    )
    qkv_rows = qkv_rows.astype(jnp.bfloat16)
    qkv_images = jnp.swapaxes(qkv_rows, 0, 1).reshape(image_count, seq_length, 3, head_count, HD)
    query_all = qkv_images[:, :, 0]
    key_all = qkv_images[:, :, 1]
    value_all = qkv_images[:, :, 2]
    attended_img, log_totals = lax.map(forward_image, (query_all, key_all, value_all, kept_all))
    attended_rows = jnp.swapaxes(attended_img.reshape(image_count, seq_length, local_width), 0, 1)
    row_block = attended_rows
    projected = lax.psum_scatter(
        jnp.einsum("sbc,cd->sbd", row_block, out_full, preferred_element_type=jnp.float32),
        "tensor",
        scatter_dimension=0,
        tiled=True,
    )
    after_attn = input_float + projected + out_shift
    normed_two = layer_norm(after_attn, gain_two, shift_two).astype(jnp.bfloat16)
    normed_all_two = lax.all_gather(normed_two, "tensor", axis=0, tiled=True)
    up_values = (
        jnp.einsum("sbd,df->sbf", normed_all_two, up_full, preferred_element_type=jnp.float32)
        + up_row
    )
    activated = gelu_exact(up_values).astype(jnp.bfloat16)
    row_block = activated
    mlp_out = lax.psum_scatter(
        jnp.einsum("sbf,fd->sbd", row_block, down_full, preferred_element_type=jnp.float32),
        "tensor",
        scatter_dimension=0,
        tiled=True,
    )
    block_output = (after_attn + mlp_out + down_shift) * kept_float
    qkv_back, out_back, up_back, down_back = (qkv_matrix, out_full, up_full, down_full)
    out_grad = cotangent * kept_float
    down_shift_grad = jnp.sum(out_grad, axis=(0, 1))
    out_low = out_grad.astype(jnp.bfloat16)
    out_low_all = lax.all_gather(out_low, "tensor", axis=0, tiled=True)
    down_weight_grad = jnp.einsum(
        "sbf,sbd->fd", activated, out_low_all, preferred_element_type=jnp.float32
    )
    act_grad = jnp.einsum("sbd,fd->sbf", out_low_all, down_back, preferred_element_type=jnp.float32)
    _, gelu_back = jax.vjp(gelu_exact, up_values)
    up_grad = gelu_back(act_grad)[0].astype(jnp.bfloat16)
    up_shift_grad = jnp.sum(up_grad.astype(jnp.float32), axis=(0, 1))
    up_weight_grad = jnp.einsum(
        "sbd,sbf->df", normed_all_two, up_grad, preferred_element_type=jnp.float32
    )
    row_block = up_grad
    normed_two_grad = lax.psum_scatter(
        jnp.einsum("sbf,df->sbd", row_block, up_back, preferred_element_type=jnp.float32),
        "tensor",
        scatter_dimension=0,
        tiled=True,
    )
    _, norm_two_back = jax.vjp(layer_norm, after_attn, gain_two, shift_two)
    attn_side, gain_two_grad, shift_two_grad = norm_two_back(normed_two_grad)
    after_attn_grad = out_grad + attn_side
    out_shift_grad = jnp.sum(after_attn_grad, axis=(0, 1))
    proj_low = after_attn_grad.astype(jnp.bfloat16)
    proj_low_all = lax.all_gather(proj_low, "tensor", axis=0, tiled=True)
    out_weight_grad = jnp.einsum(
        "sbc,sbd->cd", attended_rows, proj_low_all, preferred_element_type=jnp.float32
    )
    attended_grad = jnp.einsum(
        "sbd,cd->sbc", proj_low_all, out_back, preferred_element_type=jnp.float32
    )
    attended_grad = attended_grad.astype(jnp.bfloat16)
    attended_grad_img = jnp.swapaxes(attended_grad, 0, 1).reshape(
        image_count, seq_length, head_count, HD
    )
    qkv_grad_img = lax.map(
        backward_image, (query_all, key_all, value_all, kept_all, log_totals, attended_grad_img)
    )
    qkv_grad = jnp.swapaxes(qkv_grad_img, 0, 1)
    qkv_sums = jnp.sum(qkv_grad.astype(jnp.float32), axis=(0, 1))
    qv_grad = jnp.stack([qkv_sums[:local_width], qkv_sums[2 * local_width :]], axis=0).reshape(
        2, 1, local_width
    )
    qkv_weight_grad = jnp.einsum(
        "sbd,sbc->dc", normed_all, qkv_grad, preferred_element_type=jnp.float32
    )
    qkv_weight_grad = qkv_weight_grad.reshape(model_width, 3, local_width)
    row_block = qkv_grad
    normed_one_grad = lax.psum_scatter(
        jnp.einsum("sbc,dc->sbd", row_block, qkv_back, preferred_element_type=jnp.float32),
        "tensor",
        scatter_dimension=0,
        tiled=True,
    )
    _, norm_one_back = jax.vjp(layer_norm, input_float, gain_one, shift_one)
    input_side, gain_one_grad, shift_one_grad = norm_one_back(normed_one_grad)
    input_grad = after_attn_grad + input_side
    vector_grads = jnp.stack(
        [
            gain_one_grad,
            shift_one_grad,
            out_shift_grad,
            gain_two_grad,
            shift_two_grad,
            down_shift_grad,
        ],
        axis=0,
    ).reshape(6, tensor_count, model_width // tensor_count)
    vector_local = lax.psum_scatter(vector_grads, "tensor", scatter_dimension=1, tiled=True)
    owned = (
        lax.psum_scatter(qkv_weight_grad, "dp", scatter_dimension=0, tiled=True),
        lax.psum_scatter(out_weight_grad, "dp", scatter_dimension=1, tiled=True),
        lax.psum_scatter(up_weight_grad, "dp", scatter_dimension=0, tiled=True),
        lax.psum_scatter(down_weight_grad, "dp", scatter_dimension=1, tiled=True),
        lax.psum_scatter(qv_grad, "dp", scatter_dimension=2, tiled=True),
        lax.psum_scatter(up_shift_grad.reshape(1, -1), "dp", scatter_dimension=1, tiled=True),
        lax.psum_scatter(vector_local, "dp", scatter_dimension=2, tiled=True),
    )
    qkv_owned, out_owned, up_owned, down_owned, qv_owned, hidden_owned, vector_owned = owned
    return (
        block_output,
        input_grad,
        vector_owned[0],
        vector_owned[1],
        qkv_owned,
        qv_owned,
        out_owned,
        vector_owned[2],
        vector_owned[3],
        vector_owned[4],
        up_owned,
        hidden_owned,
        down_owned,
        vector_owned[5],
    )


NT = (((1,), (1,)), ((), ()))
NN = (((1,), (0,)), ((), ()))


def dot_nn(a, b):
    return lax.dot_general(a, b, NN, preferred_element_type=F32)


def dot_nt(a, b):
    return lax.dot_general(a, b, NT, preferred_element_type=F32)


def attention_forward_kernel(lengths, q_ref, k_ref, v_ref, o_ref, lse_ref, *, key_rows):
    length = lengths[pl.program_id(0)]
    queries = q_ref[0] * jnp.asarray(HD**-0.5, BF16)
    keys = k_ref[0, :key_rows]
    values_t = jnp.transpose(v_ref[0, :key_rows].astype(F32)).astype(BF16)
    lane = lax.broadcasted_iota(jnp.int32, (key_rows, PAIR), 1)
    valid = lax.broadcasted_iota(jnp.int32, (key_rows, q_ref.shape[1]), 0) < length
    outs = []
    for head in range(2):
        own = (lane >= head * HD) & (lane < (head + 1) * HD)
        scores = dot_nt(jnp.where(own, keys, jnp.zeros_like(keys)), queries)
        scores = jnp.where(valid, scores, masked_score)
        top = jnp.max(scores, axis=0, keepdims=True)
        exps = jnp.exp(scores - top)
        total = jnp.sum(exps, axis=0, keepdims=True)
        lse_ref[0, 0, head : head + 1, :] = top + jnp.log(total)
        probs = (exps * (1.0 / total)).astype(BF16)
        outs.append(dot_nn(values_t[head * HD : (head + 1) * HD], probs))
    o_ref[0] = jnp.transpose(jnp.concatenate(outs, axis=0)).astype(BF16)


def attention_backward_kernel(
    lengths, q_ref, k_ref, v_ref, lse_ref, g_ref, d_ref, *, key_rows
):
    length = lengths[pl.program_id(0)]
    slots = q_ref.shape[1]
    scale = HD**-0.5
    plain = q_ref[0]
    queries = plain * jnp.asarray(scale, BF16)
    keys = k_ref[0, :key_rows]
    values = v_ref[0, :key_rows]
    grads = g_ref[0]
    keys_t = jnp.transpose(keys.astype(F32)).astype(BF16)
    lane = lax.broadcasted_iota(jnp.int32, (key_rows, PAIR), 1)
    valid = lax.broadcasted_iota(jnp.int32, (key_rows, slots), 0) < length
    zero = jnp.zeros_like(keys)
    dqs, dks, dvs = [], [], []
    for head in range(2):
        own = (lane >= head * HD) & (lane < (head + 1) * HD)
        scores = dot_nt(jnp.where(own, keys, zero), queries)
        soft = jnp.where(valid, jnp.exp(scores - lse_ref[0, 0, head : head + 1, :]), 0.0)
        prob_grad = dot_nt(jnp.where(own, values, zero), grads)
        inner = jnp.sum(prob_grad * soft, axis=0, keepdims=True)
        score_grad = (soft * (prob_grad - inner)).astype(BF16)
        dvs.append(dot_nn(soft.astype(BF16), grads))
        dks.append(dot_nn(score_grad, plain))
        dqs.append(dot_nn(keys_t[head * HD : (head + 1) * HD], score_grad))
    first = lane < HD
    d_ref[0, :, :PAIR] = (jnp.transpose(jnp.concatenate(dqs, axis=0)) * scale).astype(BF16)
    d_ref[0, :key_rows, PAIR : 2 * PAIR] = (jnp.where(first, dks[0], dks[1]) * scale).astype(BF16)
    d_ref[0, :key_rows, 2 * PAIR :] = jnp.where(first, dvs[0], dvs[1]).astype(BF16)
    if key_rows < slots:
        d_ref[0, key_rows:, PAIR:] = jnp.zeros((slots - key_rows, 2 * PAIR), BF16)


def key_count(slots):
    return min(slots, -(-VALID // 16) * 16)


def pair_block(slots, each, offset):
    return pl.BlockSpec((1, slots, PAIR), lambda b, p, ln: (b, 0, each * p + offset))


def attention_forward(lengths, qkv):
    images, slots, columns = qkv.shape
    width = columns // 3
    pairs = width // PAIR
    return pl.pallas_call(
        functools.partial(attention_forward_kernel, key_rows=key_count(slots)),
        out_shape=(
            jax.ShapeDtypeStruct((images, slots, width), BF16),
            jax.ShapeDtypeStruct((images, pairs, 2, slots), F32),
        ),
        grid_spec=pltpu.PrefetchScalarGridSpec(
            num_scalar_prefetch=1,
            grid=(images, pairs),
            in_specs=[pair_block(slots, 3, n) for n in range(3)],
            out_specs=(
                pair_block(slots, 1, 0),
                pl.BlockSpec((1, 1, 2, slots), lambda b, p, ln: (b, p, 0, 0)),
            ),
        ),
        compiler_params=pltpu.CompilerParams(vmem_limit_bytes=40 << 20),
        cost_estimate=pl.CostEstimate(
            flops=images * pairs * 2 * 4 * slots * slots * PAIR,
            bytes_accessed=images * slots * width * 8,
            transcendentals=images * pairs * 2 * slots * slots,
        ),
        name="attention_forward",
    )(lengths, qkv, qkv, qkv)


def attention_backward(lengths, qkv, lse, grads):
    images, slots, columns = qkv.shape
    width = columns // 3
    pairs = width // PAIR
    return pl.pallas_call(
        functools.partial(attention_backward_kernel, key_rows=key_count(slots)),
        out_shape=jax.ShapeDtypeStruct(qkv.shape, BF16),
        grid_spec=pltpu.PrefetchScalarGridSpec(
            num_scalar_prefetch=1,
            grid=(images, pairs),
            in_specs=[pair_block(slots, 3, n) for n in range(3)]
            + [
                pl.BlockSpec((1, 1, 2, slots), lambda b, p, ln: (b, p, 0, 0)),
                pair_block(slots, 1, 0),
            ],
            out_specs=pl.BlockSpec((1, slots, 3 * PAIR), lambda b, p, ln: (b, 0, p)),
        ),
        compiler_params=pltpu.CompilerParams(vmem_limit_bytes=40 << 20),
        cost_estimate=pl.CostEstimate(
            flops=images * pairs * 2 * 10 * slots * slots * PAIR,
            bytes_accessed=images * slots * width * 14,
            transcendentals=images * pairs * 2 * slots * slots,
        ),
        name="attention_backward",
    )(lengths, qkv, qkv, qkv, lse, grads)


def swap(array, axis, step):
    return lax.ppermute(array, axis, [(n, n ^ step) for n in range(lax.axis_size(axis))])


def shift(array, groups, by):
    count = 4 * groups
    return lax.ppermute(array, "dp", [(n, (n + 4 * by) % count) for n in range(count)])


def place():
    index = lax.axis_index("dp")
    return jnp.stack(
        [lax.axis_index("tensor"), index // 4, (index // 2) % 2, index % 2]
    ).astype(jnp.int32)


def assemble_kernel(where, *refs, groups, columns):
    *sources, out_ref, extra_ref, sems = refs
    t, z, x, c = [where[n] for n in range(4)]
    half = sources[0].shape[2]
    tail = extra_ref.shape[4]
    copies = []

    def move(source, target):
        copies.append(pltpu.make_async_copy(source, target, sems.at[len(copies)]))
        copies[-1].start()

    for turn in range(2):
        for kind in range(4):
            source = sources[4 * turn + kind]
            for near in range(2):
                for ahead in range(groups):
                    far = kind % 2
                    along_t, along_x = (far, near) if kind < 2 else (near, far)
                    rows = pl.ds((kind // 2) * half, half)
                    origin = lax.rem(z + groups - ahead, groups), x ^ along_x, c ^ turn
                    side = t ^ along_t
                    start = pl.multiple_of(side * columns, 128)
                    move(
                        source.at[near, ahead, :, pl.ds(0, columns)],
                        out_ref.at[(*origin, rows, pl.ds(start, columns))],
                    )
                    if kind < 2:
                        move(
                            source.at[near, ahead, pl.ds(0, tail), pl.ds(columns, 128)],
                            extra_ref.at[(side, *origin)],
                        )
    for copy in copies:
        copy.wait()


def gather_staged(shard, vector, coords):
    rows, columns = shard.shape
    groups = lax.axis_size("dp") // 4
    entries = vector.shape[0]
    tail = 16
    beside = jnp.zeros((rows * 128,), BF16).at[:entries].set(vector).reshape(rows, 128)
    shard = jnp.concatenate([shard, beside], axis=1)
    line = jnp.stack([shard] + [shift(shard, groups, by) for by in range(1, groups)])
    upper, lower = line[:, : rows // 2], line[:, rows // 2 :]
    upper = jnp.stack([upper, swap(upper, "dp", 2)])
    lower = jnp.stack([lower, swap(lower, "tensor", 1)])
    mine = [upper, swap(upper, "tensor", 1), lower, swap(lower, "dp", 2)]
    theirs = [swap(piece, "dp", 1) for piece in mine]
    anywhere = pl.BlockSpec(memory_space=pl.ANY)
    inside = pl.BlockSpec(memory_space=pltpu.VMEM)
    whole, extra = pl.pallas_call(
        functools.partial(assemble_kernel, groups=groups, columns=columns),
        out_shape=(
            jax.ShapeDtypeStruct((groups, 2, 2, rows, 2 * columns), BF16),
            jax.ShapeDtypeStruct((2, groups, 2, 2, tail, 128), BF16),
        ),
        grid_spec=pltpu.PrefetchScalarGridSpec(
            num_scalar_prefetch=1,
            in_specs=[anywhere] * 8,
            out_specs=(inside, inside),
            scratch_shapes=[pltpu.SemaphoreType.DMA((24 * groups,))],
        ),
        compiler_params=pltpu.CompilerParams(vmem_limit_bytes=(4 << 20) + 16 * groups * rows * columns),
        cost_estimate=pl.CostEstimate(
            flops=0, transcendentals=0, bytes_accessed=32 * groups * rows * columns
        ),
        name="assemble",
    )(coords, *mine, *theirs)
    extra = extra.reshape(2, 4 * groups, tail * 128)[:, :, :entries]
    return whole.reshape(4 * groups * rows, 2 * columns), extra


def beside_kernel(source, out_ref, sems, *, offset, columns):
    copies = [
        pltpu.make_async_copy(
            source.at[t, :, pl.ds(offset, columns)],
            out_ref.at[:, pl.ds(t * columns, columns)],
            sems.at[t],
        )
        for t in range(2)
    ]
    for copy in copies:
        copy.start()
    for copy in copies:
        copy.wait()


def beside(gathered, offset, columns):
    rows = gathered.shape[1]
    return pl.pallas_call(
        functools.partial(beside_kernel, offset=offset, columns=columns),
        out_shape=jax.ShapeDtypeStruct((rows, 2 * columns), BF16),
        in_specs=[pl.BlockSpec(memory_space=pl.ANY)],
        out_specs=pl.BlockSpec(memory_space=pltpu.VMEM),
        scratch_shapes=[pltpu.SemaphoreType.DMA((2,))],
        compiler_params=pltpu.CompilerParams(vmem_limit_bytes=(4 << 20) + 4 * rows * columns),
        cost_estimate=pl.CostEstimate(flops=0, transcendentals=0, bytes_accessed=8 * rows * columns),
        name="beside",
    )(gathered)


def take(array, index, axis):
    return lax.dynamic_index_in_dim(array, index, axis, keepdims=False)


def side(array, index):
    half = array.shape[-1] // 2
    return lax.dynamic_slice_in_dim(array, index * half, half, array.ndim - 1)


class Sum:
    def __init__(self, whole, coords, sent=BF16):
        self.t, self.z, self.x, self.c = [coords[n] for n in range(4)]
        self.groups = lax.axis_size("dp") // 4
        self.rows = whole.shape[0] // (4 * self.groups)
        self.sent = sent
        self.state = [whole.reshape(self.groups, 2, 2, self.rows, whole.shape[1])]
        self.stage = 0

    def over_tensor(self, array):
        return side(array, self.t) + swap(side(array, 1 - self.t).astype(self.sent), "tensor", 1).astype(F32)

    def over_pair(self, array, mine, dim, step):
        return take(array, mine, dim) + swap(take(array, 1 - mine, dim).astype(self.sent), "dp", step).astype(F32)

    def step(self):
        half = self.rows // 2
        if self.stage == 0:
            self.state = [self.over_pair(self.state[0], self.c, 2, 1)]
        elif self.stage == 1:
            whole = self.state[0]
            self.state = [
                self.over_tensor(whole[:, :, :half]),
                self.over_pair(whole[:, :, half:], self.x, 1, 2),
            ]
        elif self.stage == 2:
            upper, lower = self.state
            self.state = [self.over_pair(upper, self.x, 1, 2), self.over_tensor(lower)]
        elif self.stage == 3:
            line = jnp.concatenate(self.state, axis=1)
            total = take(line, self.z, 0)
            for by in range(1, self.groups):
                sent = take(line, lax.rem(self.z + by, self.groups), 0).astype(self.sent)
                total = total + shift(sent, self.groups, by).astype(F32)
            self.state = [total]
        self.stage += 1

    def result(self):
        while self.stage < 4:
            self.step()
        return self.state[0]


def advance(sums, *values):
    for one in sums:
        one.step()
    states = [one.state for one in sums]
    values, states = lax.optimization_barrier((values, states))
    for one, state in zip(sums, states):
        one.state = state
    return values if len(values) > 1 else values[0]


def to_images(rows):
    me = lax.axis_index("tensor")
    own, part = rows.shape[0] // 2, rows.shape[1]
    kept = lax.dynamic_slice_in_dim(rows, me * own, own, 0)
    sent = lax.dynamic_slice_in_dim(rows, (1 - me) * own, own, 0)
    came = lax.ppermute(sent, "tensor", [(0, 1), (1, 0)])
    whole = jnp.zeros((own, 2 * part) + rows.shape[2:], rows.dtype)
    whole = lax.dynamic_update_slice_in_dim(whole, kept, me * part, 1)
    return lax.dynamic_update_slice_in_dim(whole, came, (1 - me) * part, 1)


def to_slots(rows):
    me = lax.axis_index("tensor")
    own, part = rows.shape[0], rows.shape[1] // 2
    kept = lax.dynamic_slice_in_dim(rows, me * part, part, 1)
    sent = lax.dynamic_slice_in_dim(rows, (1 - me) * part, part, 1).astype(BF16)
    came = lax.ppermute(sent, "tensor", [(0, 1), (1, 0)]).astype(rows.dtype)
    first = jnp.where(me == 0, kept, came)
    second = jnp.where(me == 0, came, kept)
    return jnp.swapaxes(jnp.concatenate([first, second], axis=0), 0, 1)


def normalize(values):
    row_mean = jnp.mean(values, axis=-1, keepdims=True)
    centred = values - row_mean
    spread = jnp.mean(centred * centred, axis=-1, keepdims=True)
    inverse = lax.rsqrt(spread + epsilon)
    return centred * inverse, inverse


def normalize_back(grad, unit, inverse, gain):
    scaled = grad * gain
    mean_one = jnp.mean(scaled, axis=-1, keepdims=True)
    mean_two = jnp.mean(scaled * unit, axis=-1, keepdims=True)
    return inverse * (scaled - mean_one - unit * mean_two)


def gelu_pair(values):
    area = 0.5 * (1.0 + lax.erf(values * (0.5**0.5)))
    density = jnp.exp(-0.5 * values * values) * ((2.0 * jnp.pi) ** -0.5)
    return (values * area).astype(BF16), area + values * density


def token_sum(values):
    return jnp.sum(values.astype(F32), axis=(0, 1))


def by_images(
    inputs,
    pad_mask,
    norm1_gain,
    norm1_shift,
    qkv_weight,
    qv_bias,
    out_weight,
    out_bias,
    norm2_gain,
    norm2_shift,
    up_weight,
    up_bias,
    down_weight,
    down_bias,
    cotangent,
):
    width = inputs.shape[2]
    me = lax.axis_index("tensor")
    images = inputs.shape[1] // 2
    head_width = qkv_weight.shape[2]
    pairs = head_width // PAIR
    hidden = up_weight.shape[1]
    piece = norm1_gain.shape[1]
    depth = qkv_weight.shape[0]
    coords = place()
    product = functools.partial(jnp.einsum, preferred_element_type=F32)

    x = to_images(jnp.swapaxes(inputs, 0, 1)).astype(F32)
    vector = jnp.concatenate(
        [
            v.reshape(-1)
            for v in (norm1_gain, norm1_shift, out_bias, norm2_gain, norm2_shift, down_bias, qv_bias, up_bias)
        ]
    )
    paired = jnp.swapaxes(qkv_weight.reshape(depth, 3, pairs, PAIR), 1, 2).reshape(depth, -1)
    qkv_full, flat = gather_staged(paired, vector, coords)
    flat = flat.astype(F32)
    gain_one, shift_one, out_shift, gain_two, shift_two, down_shift = [
        flat[:, :, n * piece : (n + 1) * piece].reshape(width) for n in range(6)
    ]
    query_bias = flat[:, :, 6 * piece : 7 * piece].reshape(2 * pairs, PAIR)
    value_bias = flat[:, :, 7 * piece : 8 * piece].reshape(2 * pairs, PAIR)
    qkv_bias = jnp.stack([query_bias, jnp.zeros_like(query_bias), value_bias], axis=1).reshape(-1)
    up_row = flat[:, :, 8 * piece :].reshape(2 * hidden)

    others = jnp.concatenate([jnp.transpose(out_weight), up_weight, jnp.transpose(down_weight)], axis=1)
    others = lax.all_gather(others, ("tensor", "dp"), axis=0, tiled=True).reshape(2, width, -1)
    out_full = beside(others, 0, head_width)
    up_full = beside(others, head_width, hidden)
    down_full = beside(others, head_width + hidden, hidden)

    here = lax.dynamic_slice_in_dim(pad_mask, me * inputs.shape[0], inputs.shape[0], 1) > 0
    down_shift_grad = token_sum(cotangent * jnp.transpose(here).astype(F32)[:, :, None])
    mask = lax.dynamic_slice_in_dim(pad_mask, me * images, images, 0)
    lengths = jnp.sum(mask, axis=1).astype(jnp.int32)
    kept = (mask > 0).astype(F32)[:, :, None]

    unit_one, inverse_one = normalize(x)
    normed_one = (unit_one * gain_one + shift_one).astype(BF16)
    qkv = (product("bsd,dc->bsc", normed_one, qkv_full) + qkv_bias).astype(BF16)
    cotangent, qkv = lax.optimization_barrier((cotangent, qkv))
    cot = to_images(jnp.swapaxes(cotangent.astype(BF16), 0, 1)).astype(F32)
    attended, lse = attention_forward(lengths, qkv)
    projected = product("bsc,dc->bsd", attended, out_full)
    after_attn = x + projected + out_shift
    unit_two, inverse_two = normalize(after_attn)
    normed_two = (unit_two * gain_two + shift_two).astype(BF16)
    up_values = product("bsd,df->bsf", normed_two, up_full) + up_row
    act, slope = gelu_pair(up_values)
    out_low = (cot * kept).astype(BF16)
    out_grad = out_low.astype(F32)

    down = Sum(product("bsd,bsf->df", out_low, act), coords)
    (out_low,), (down.state,) = lax.optimization_barrier(((out_low,), (down.state,)))
    act_grad = product("bsd,df->bsf", out_low, down_full)
    up_grad = (act_grad * slope).astype(BF16)
    up_grad, normed_two = advance([down], up_grad, normed_two)
    up = Sum(product("bsd,bsf->df", normed_two, up_grad), coords)
    up_shift_grad = token_sum(up_grad)
    down.step()
    (up_grad,), (down.state, up.state) = lax.optimization_barrier(((up_grad,), (down.state, up.state)))
    normed_two_grad = product("bsf,df->bsd", up_grad, up_full)
    normed_two_grad = advance([down, up], normed_two_grad)
    gain_two_grad = token_sum(normed_two_grad * unit_two)
    shift_two_grad = token_sum(normed_two_grad)
    after_attn_grad = out_grad + normalize_back(normed_two_grad, unit_two, inverse_two, gain_two)
    out_shift_grad = token_sum(after_attn_grad)
    proj_low = after_attn_grad.astype(BF16)
    out = Sum(product("bsd,bsc->dc", proj_low, attended), coords)
    attended_grad = product("bsd,dc->bsc", proj_low, out_full).astype(BF16)
    down.step()
    up.step()
    (attended_grad, qkv), (down.state, up.state, out.state) = lax.optimization_barrier(
        ((attended_grad, qkv), (down.state, up.state, out.state))
    )
    qkv_grad = attention_backward(lengths, qkv, lse, attended_grad)
    qkv_grad, normed_one = advance([up, out], qkv_grad, normed_one)
    qkv_sum = Sum(product("bsd,bsc->dc", normed_one, qkv_grad), coords)
    up.step()
    out.step()
    (qkv_grad, act), (up.state, out.state, qkv_sum.state) = lax.optimization_barrier(
        ((qkv_grad, act), (up.state, out.state, qkv_sum.state))
    )
    mlp_out = product("bsf,df->bsd", act, down_full)
    mlp_out, qkv_grad = advance([out, qkv_sum], mlp_out, qkv_grad)
    block_output = to_slots((after_attn + mlp_out + down_shift) * kept)
    normed_one_grad = product("bsc,dc->bsd", qkv_grad, qkv_full)
    bias_sums = token_sum(qkv_grad).reshape(2 * pairs, 3, PAIR)
    normed_one_grad = advance([out, qkv_sum], normed_one_grad)
    gain_one_grad = token_sum(normed_one_grad * unit_one)
    shift_one_grad = token_sum(normed_one_grad)
    input_grad = after_attn_grad + normalize_back(normed_one_grad, unit_one, inverse_one, gain_one)
    input_grad = to_slots(input_grad)

    vectors = [gain_one_grad, shift_one_grad, out_shift_grad, gain_two_grad, shift_two_grad, down_shift_grad]
    vectors += [bias_sums[:, 0], bias_sums[:, 2], up_shift_grad]
    small = jnp.concatenate([v.reshape(2, lax.axis_size("dp"), -1) for v in vectors], axis=2)
    entries = small.shape[2]
    small = jnp.swapaxes(small.reshape(2, -1, entries // 2), 0, 1).reshape(-1, entries)
    small = Sum(small, coords, F32).result().reshape(1, entries)
    row = lambda n: small[:, n * piece : (n + 1) * piece]
    qkv_owned = jnp.swapaxes(qkv_sum.result().reshape(depth, pairs, 3, PAIR), 1, 2)
    return (
        block_output,
        input_grad,
        row(0),
        row(1),
        qkv_owned.reshape(qkv_weight.shape),
        jnp.stack([row(6), row(7)], axis=0),
        jnp.transpose(out.result()),
        row(2),
        row(3),
        row(4),
        up.result(),
        small[:, 8 * piece :],
        jnp.transpose(down.result()),
        row(5),
    )


def solution(mesh):
    in_specs = (
        P("tensor", "dp", None),
        P("dp", None),
        P("tensor", "dp"),
        P("tensor", "dp"),
        P("dp", None, "tensor"),
        P(None, "tensor", "dp"),
        P("tensor", "dp"),
        P("tensor", "dp"),
        P("tensor", "dp"),
        P("tensor", "dp"),
        P("dp", "tensor"),
        P("tensor", "dp"),
        P("tensor", "dp"),
        P("tensor", "dp"),
        P("tensor", "dp", None),
    )
    out_specs = (
        P("tensor", "dp", None),
        P("tensor", "dp", None),
        P("tensor", "dp"),
        P("tensor", "dp"),
        P("dp", None, "tensor"),
        P(None, "tensor", "dp"),
        P("tensor", "dp"),
        P("tensor", "dp"),
        P("tensor", "dp"),
        P("tensor", "dp"),
        P("dp", "tensor"),
        P("tensor", "dp"),
        P("tensor", "dp"),
        P("tensor", "dp"),
    )
    dims = dict(zip(mesh.axis_names, mesh.devices.shape))

    def choose(inputs, *rest):
        whole_images = dims["tensor"] == 2 and dims["dp"] % 4 == 0 and inputs.shape[1] % 2 == 0
        return (by_images if whole_images else on_device)(inputs, *rest)

    return jax.shard_map(
        choose, mesh=mesh, in_specs=in_specs, out_specs=out_specs, check_vma=False
    )
```

```python
import functools

import jax
import jax.numpy as jnp
from jax import lax
from jax.experimental import pallas as pl
from jax.experimental.pallas import tpu as pltpu
from jax.sharding import PartitionSpec as P

HD = 64
PAIR = 2 * HD
VALID = 577
F32 = jnp.float32
BF16 = jnp.bfloat16

epsilon = 1e-06
masked_score = -1e30


def layer_norm(values, gain, shift):
    row_mean = jnp.mean(values, axis=-1, keepdims=True)
    centred = values - row_mean
    spread = jnp.mean(centred * centred, axis=-1, keepdims=True)
    return centred * lax.rsqrt(spread + epsilon) * gain + shift


def gelu_exact(values):
    return jax.nn.gelu(values, approximate=False)


def image_scores(queries, key_rows, kept_row):
    scores = jnp.einsum(
        "qhe,khe->hqk", queries, key_rows, preferred_element_type=jnp.float32
    ) * HD ** (-0.5)
    return jnp.where(kept_row[None, None, :], scores, masked_score)


def forward_image(operands):
    queries, key_rows, value_rows, kept_row = operands
    scores = image_scores(queries, key_rows, kept_row)
    row_max = jnp.max(scores, axis=-1, keepdims=True)
    exps = jnp.exp(scores - row_max)
    row_total = jnp.sum(exps, axis=-1, keepdims=True)
    soft_weights = (exps / row_total).astype(jnp.bfloat16)
    attended = jnp.einsum(
        "hqk,khe->qhe", soft_weights, value_rows, preferred_element_type=jnp.float32
    )
    return (attended.astype(jnp.bfloat16), (row_max + jnp.log(row_total))[..., 0])


def backward_image(operands):
    queries, key_rows, value_rows, kept_row, log_total, attended_grad = operands
    seq_length = queries.shape[0]
    scores = image_scores(queries, key_rows, kept_row)
    soft_float = jnp.exp(scores - log_total[..., None])
    soft_weights = soft_float.astype(jnp.bfloat16)
    value_grad = jnp.einsum(
        "hqk,qhe->khe", soft_weights, attended_grad, preferred_element_type=jnp.float32
    )
    prob_grad = jnp.einsum(
        "qhe,khe->hqk", attended_grad, value_rows, preferred_element_type=jnp.float32
    )
    score_grad = soft_float * (prob_grad - jnp.sum(prob_grad * soft_float, axis=-1, keepdims=True))
    score_grad = score_grad.astype(jnp.bfloat16)
    query_grad = jnp.einsum(
        "hqk,khe->qhe", score_grad, key_rows, preferred_element_type=jnp.float32
    ) * HD ** (-0.5)
    key_grad = jnp.einsum(
        "hqk,qhe->khe", score_grad, queries, preferred_element_type=jnp.float32
    ) * HD ** (-0.5)
    joined = jnp.concatenate(
        [
            query_grad.reshape(seq_length, -1),
            key_grad.reshape(seq_length, -1),
            value_grad.reshape(seq_length, -1),
        ],
        axis=-1,
    )
    return joined.astype(jnp.bfloat16)


def on_device(
    inputs,
    pad_mask,
    norm1_gain,
    norm1_shift,
    qkv_weight,
    qv_bias,
    out_weight,
    out_bias,
    norm2_gain,
    norm2_shift,
    up_weight,
    up_bias,
    down_weight,
    down_bias,
    cotangent,
):
    local_rows = inputs.shape[0]
    image_count = inputs.shape[1]
    model_width = inputs.shape[2]
    seq_length = pad_mask.shape[1]
    tensor_count = lax.axis_size("tensor")
    vector_stack = jnp.stack(
        [norm1_gain, norm1_shift, out_bias, norm2_gain, norm2_shift, down_bias], axis=0
    )
    gathered = (
        lax.all_gather(qkv_weight, "dp", axis=0, tiled=True),
        lax.all_gather(out_weight, "dp", axis=1, tiled=True),
        lax.all_gather(up_weight, "dp", axis=0, tiled=True),
        lax.all_gather(down_weight, "dp", axis=1, tiled=True),
        lax.all_gather(qv_bias, "dp", axis=2, tiled=True),
        lax.all_gather(up_bias, "dp", axis=1, tiled=True),
        lax.all_gather(vector_stack, "dp", axis=2, tiled=True),
    )
    qkv_full, out_full, up_full, down_full, bias_pair, bias_hidden, vector_part = gathered
    local_width = qkv_full.shape[2]
    head_count = local_width // HD
    vector_rows = (
        lax.all_gather(vector_part, "tensor", axis=1, tiled=True)
        .reshape(6, model_width)
        .astype(jnp.float32)
    )
    gain_one, shift_one, out_shift, gain_two, shift_two, down_shift = [
        vector_rows[index] for index in range(6)
    ]
    qkv_matrix = qkv_full.reshape(model_width, 3 * local_width)
    bias_row = jnp.concatenate(
        [
            bias_pair[0, 0].astype(jnp.float32),
            jnp.zeros((local_width,), jnp.float32),
            bias_pair[1, 0].astype(jnp.float32),
        ]
    )
    up_row = bias_hidden.reshape(-1).astype(jnp.float32)
    kept_all = pad_mask > 0
    first_row = lax.axis_index("tensor") * local_rows
    kept_float = jnp.transpose(lax.dynamic_slice_in_dim(kept_all, first_row, local_rows, 1)).astype(
        jnp.float32
    )[:, :, None]
    input_float = inputs.astype(jnp.float32)
    normed_one = layer_norm(input_float, gain_one, shift_one).astype(jnp.bfloat16)
    normed_all = lax.all_gather(normed_one, "tensor", axis=0, tiled=True)
    qkv_rows = (
        jnp.einsum("sbd,dc->sbc", normed_all, qkv_matrix, preferred_element_type=jnp.float32)
        + bias_row
    )
    qkv_rows = qkv_rows.astype(jnp.bfloat16)
    qkv_images = jnp.swapaxes(qkv_rows, 0, 1).reshape(image_count, seq_length, 3, head_count, HD)
    query_all = qkv_images[:, :, 0]
    key_all = qkv_images[:, :, 1]
    value_all = qkv_images[:, :, 2]
    attended_img, log_totals = lax.map(forward_image, (query_all, key_all, value_all, kept_all))
    attended_rows = jnp.swapaxes(attended_img.reshape(image_count, seq_length, local_width), 0, 1)
    row_block = attended_rows
    projected = lax.psum_scatter(
        jnp.einsum("sbc,cd->sbd", row_block, out_full, preferred_element_type=jnp.float32),
        "tensor",
        scatter_dimension=0,
        tiled=True,
    )
    after_attn = input_float + projected + out_shift
    normed_two = layer_norm(after_attn, gain_two, shift_two).astype(jnp.bfloat16)
    normed_all_two = lax.all_gather(normed_two, "tensor", axis=0, tiled=True)
    up_values = (
        jnp.einsum("sbd,df->sbf", normed_all_two, up_full, preferred_element_type=jnp.float32)
        + up_row
    )
    activated = gelu_exact(up_values).astype(jnp.bfloat16)
    row_block = activated
    mlp_out = lax.psum_scatter(
        jnp.einsum("sbf,fd->sbd", row_block, down_full, preferred_element_type=jnp.float32),
        "tensor",
        scatter_dimension=0,
        tiled=True,
    )
    block_output = (after_attn + mlp_out + down_shift) * kept_float
    qkv_back, out_back, up_back, down_back = (qkv_matrix, out_full, up_full, down_full)
    out_grad = cotangent * kept_float
    down_shift_grad = jnp.sum(out_grad, axis=(0, 1))
    out_low = out_grad.astype(jnp.bfloat16)
    out_low_all = lax.all_gather(out_low, "tensor", axis=0, tiled=True)
    down_weight_grad = jnp.einsum(
        "sbf,sbd->fd", activated, out_low_all, preferred_element_type=jnp.float32
    )
    act_grad = jnp.einsum("sbd,fd->sbf", out_low_all, down_back, preferred_element_type=jnp.float32)
    _, gelu_back = jax.vjp(gelu_exact, up_values)
    up_grad = gelu_back(act_grad)[0].astype(jnp.bfloat16)
    up_shift_grad = jnp.sum(up_grad.astype(jnp.float32), axis=(0, 1))
    up_weight_grad = jnp.einsum(
        "sbd,sbf->df", normed_all_two, up_grad, preferred_element_type=jnp.float32
    )
    row_block = up_grad
    normed_two_grad = lax.psum_scatter(
        jnp.einsum("sbf,df->sbd", row_block, up_back, preferred_element_type=jnp.float32),
        "tensor",
        scatter_dimension=0,
        tiled=True,
    )
    _, norm_two_back = jax.vjp(layer_norm, after_attn, gain_two, shift_two)
    attn_side, gain_two_grad, shift_two_grad = norm_two_back(normed_two_grad)
    after_attn_grad = out_grad + attn_side
    out_shift_grad = jnp.sum(after_attn_grad, axis=(0, 1))
    proj_low = after_attn_grad.astype(jnp.bfloat16)
    proj_low_all = lax.all_gather(proj_low, "tensor", axis=0, tiled=True)
    out_weight_grad = jnp.einsum(
        "sbc,sbd->cd", attended_rows, proj_low_all, preferred_element_type=jnp.float32
    )
    attended_grad = jnp.einsum(
        "sbd,cd->sbc", proj_low_all, out_back, preferred_element_type=jnp.float32
    )
    attended_grad = attended_grad.astype(jnp.bfloat16)
    attended_grad_img = jnp.swapaxes(attended_grad, 0, 1).reshape(
        image_count, seq_length, head_count, HD
    )
    qkv_grad_img = lax.map(
        backward_image, (query_all, key_all, value_all, kept_all, log_totals, attended_grad_img)
    )
    qkv_grad = jnp.swapaxes(qkv_grad_img, 0, 1)
    qkv_sums = jnp.sum(qkv_grad.astype(jnp.float32), axis=(0, 1))
    qv_grad = jnp.stack([qkv_sums[:local_width], qkv_sums[2 * local_width :]], axis=0).reshape(
        2, 1, local_width
    )
    qkv_weight_grad = jnp.einsum(
        "sbd,sbc->dc", normed_all, qkv_grad, preferred_element_type=jnp.float32
    )
    qkv_weight_grad = qkv_weight_grad.reshape(model_width, 3, local_width)
    row_block = qkv_grad
    normed_one_grad = lax.psum_scatter(
        jnp.einsum("sbc,dc->sbd", row_block, qkv_back, preferred_element_type=jnp.float32),
        "tensor",
        scatter_dimension=0,
        tiled=True,
    )
    _, norm_one_back = jax.vjp(layer_norm, input_float, gain_one, shift_one)
    input_side, gain_one_grad, shift_one_grad = norm_one_back(normed_one_grad)
    input_grad = after_attn_grad + input_side
    vector_grads = jnp.stack(
        [
            gain_one_grad,
            shift_one_grad,
            out_shift_grad,
            gain_two_grad,
            shift_two_grad,
            down_shift_grad,
        ],
        axis=0,
    ).reshape(6, tensor_count, model_width // tensor_count)
    vector_local = lax.psum_scatter(vector_grads, "tensor", scatter_dimension=1, tiled=True)
    owned = (
        lax.psum_scatter(qkv_weight_grad, "dp", scatter_dimension=0, tiled=True),
        lax.psum_scatter(out_weight_grad, "dp", scatter_dimension=1, tiled=True),
        lax.psum_scatter(up_weight_grad, "dp", scatter_dimension=0, tiled=True),
        lax.psum_scatter(down_weight_grad, "dp", scatter_dimension=1, tiled=True),
        lax.psum_scatter(qv_grad, "dp", scatter_dimension=2, tiled=True),
        lax.psum_scatter(up_shift_grad.reshape(1, -1), "dp", scatter_dimension=1, tiled=True),
        lax.psum_scatter(vector_local, "dp", scatter_dimension=2, tiled=True),
    )
    qkv_owned, out_owned, up_owned, down_owned, qv_owned, hidden_owned, vector_owned = owned
    return (
        block_output,
        input_grad,
        vector_owned[0],
        vector_owned[1],
        qkv_owned,
        qv_owned,
        out_owned,
        vector_owned[2],
        vector_owned[3],
        vector_owned[4],
        up_owned,
        hidden_owned,
        down_owned,
        vector_owned[5],
    )


NT = (((1,), (1,)), ((), ()))
NN = (((1,), (0,)), ((), ()))


def dot_nn(a, b):
    return lax.dot_general(a, b, NN, preferred_element_type=F32)


def dot_nt(a, b):
    return lax.dot_general(a, b, NT, preferred_element_type=F32)


def attention_forward_kernel(lengths, q_ref, k_ref, v_ref, o_ref, lse_ref, *, key_rows):
    length = lengths[pl.program_id(0)]
    queries = q_ref[0] * jnp.asarray(HD**-0.5, BF16)
    keys = k_ref[0, :key_rows]
    values_t = jnp.transpose(v_ref[0, :key_rows].astype(F32)).astype(BF16)
    lane = lax.broadcasted_iota(jnp.int32, (key_rows, PAIR), 1)
    valid = lax.broadcasted_iota(jnp.int32, (key_rows, q_ref.shape[1]), 0) < length
    outs = []
    for head in range(2):
        own = (lane >= head * HD) & (lane < (head + 1) * HD)
        scores = dot_nt(jnp.where(own, keys, jnp.zeros_like(keys)), queries)
        scores = jnp.where(valid, scores, masked_score)
        top = jnp.max(scores, axis=0, keepdims=True)
        exps = jnp.exp(scores - top)
        total = jnp.sum(exps, axis=0, keepdims=True)
        lse_ref[0, 0, head : head + 1, :] = top + jnp.log(total)
        probs = (exps * (1.0 / total)).astype(BF16)
        outs.append(dot_nn(values_t[head * HD : (head + 1) * HD], probs))
    o_ref[0] = jnp.transpose(jnp.concatenate(outs, axis=0)).astype(BF16)


def attention_backward_kernel(
    lengths, q_ref, k_ref, v_ref, lse_ref, g_ref, d_ref, *, key_rows
):
    length = lengths[pl.program_id(0)]
    slots = q_ref.shape[1]
    scale = HD**-0.5
    plain = q_ref[0]
    queries = plain * jnp.asarray(scale, BF16)
    keys = k_ref[0, :key_rows]
    values = v_ref[0, :key_rows]
    grads = g_ref[0]
    keys_t = jnp.transpose(keys.astype(F32)).astype(BF16)
    lane = lax.broadcasted_iota(jnp.int32, (key_rows, PAIR), 1)
    valid = lax.broadcasted_iota(jnp.int32, (key_rows, slots), 0) < length
    zero = jnp.zeros_like(keys)
    dqs, dks, dvs = [], [], []
    for head in range(2):
        own = (lane >= head * HD) & (lane < (head + 1) * HD)
        scores = dot_nt(jnp.where(own, keys, zero), queries)
        soft = jnp.where(valid, jnp.exp(scores - lse_ref[0, 0, head : head + 1, :]), 0.0)
        prob_grad = dot_nt(jnp.where(own, values, zero), grads)
        inner = jnp.sum(prob_grad * soft, axis=0, keepdims=True)
        score_grad = (soft * (prob_grad - inner)).astype(BF16)
        dvs.append(dot_nn(soft.astype(BF16), grads))
        dks.append(dot_nn(score_grad, plain))
        dqs.append(dot_nn(keys_t[head * HD : (head + 1) * HD], score_grad))
    first = lane < HD
    d_ref[0, :, :PAIR] = (jnp.transpose(jnp.concatenate(dqs, axis=0)) * scale).astype(BF16)
    d_ref[0, :key_rows, PAIR : 2 * PAIR] = (jnp.where(first, dks[0], dks[1]) * scale).astype(BF16)
    d_ref[0, :key_rows, 2 * PAIR :] = jnp.where(first, dvs[0], dvs[1]).astype(BF16)
    if key_rows < slots:
        d_ref[0, key_rows:, PAIR:] = jnp.zeros((slots - key_rows, 2 * PAIR), BF16)


def key_count(slots):
    return min(slots, -(-VALID // 16) * 16)


def pair_block(slots, each, offset):
    return pl.BlockSpec((1, slots, PAIR), lambda b, p, ln: (b, 0, each * p + offset))


def attention_forward(lengths, qkv):
    images, slots, columns = qkv.shape
    width = columns // 3
    pairs = width // PAIR
    return pl.pallas_call(
        functools.partial(attention_forward_kernel, key_rows=key_count(slots)),
        out_shape=(
            jax.ShapeDtypeStruct((images, slots, width), BF16),
            jax.ShapeDtypeStruct((images, pairs, 2, slots), F32),
        ),
        grid_spec=pltpu.PrefetchScalarGridSpec(
            num_scalar_prefetch=1,
            grid=(images, pairs),
            in_specs=[pair_block(slots, 3, n) for n in range(3)],
            out_specs=(
                pair_block(slots, 1, 0),
                pl.BlockSpec((1, 1, 2, slots), lambda b, p, ln: (b, p, 0, 0)),
            ),
        ),
        compiler_params=pltpu.CompilerParams(vmem_limit_bytes=40 << 20),
        cost_estimate=pl.CostEstimate(
            flops=images * pairs * 2 * 4 * slots * slots * PAIR,
            bytes_accessed=images * slots * width * 8,
            transcendentals=images * pairs * 2 * slots * slots,
        ),
        name="attention_forward",
    )(lengths, qkv, qkv, qkv)


def attention_backward(lengths, qkv, lse, grads):
    images, slots, columns = qkv.shape
    width = columns // 3
    pairs = width // PAIR
    return pl.pallas_call(
        functools.partial(attention_backward_kernel, key_rows=key_count(slots)),
        out_shape=jax.ShapeDtypeStruct(qkv.shape, BF16),
        grid_spec=pltpu.PrefetchScalarGridSpec(
            num_scalar_prefetch=1,
            grid=(images, pairs),
            in_specs=[pair_block(slots, 3, n) for n in range(3)]
            + [
                pl.BlockSpec((1, 1, 2, slots), lambda b, p, ln: (b, p, 0, 0)),
                pair_block(slots, 1, 0),
            ],
            out_specs=pl.BlockSpec((1, slots, 3 * PAIR), lambda b, p, ln: (b, 0, p)),
        ),
        compiler_params=pltpu.CompilerParams(vmem_limit_bytes=40 << 20),
        cost_estimate=pl.CostEstimate(
            flops=images * pairs * 2 * 10 * slots * slots * PAIR,
            bytes_accessed=images * slots * width * 14,
            transcendentals=images * pairs * 2 * slots * slots,
        ),
        name="attention_backward",
    )(lengths, qkv, qkv, qkv, lse, grads)


def swap(array, axis, step):
    return lax.ppermute(array, axis, [(n, n ^ step) for n in range(lax.axis_size(axis))])


def shift(array, groups, by):
    count = 4 * groups
    return lax.ppermute(array, "dp", [(n, (n + 4 * by) % count) for n in range(count)])


def place():
    index = lax.axis_index("dp")
    return jnp.stack(
        [lax.axis_index("tensor"), index // 4, (index // 2) % 2, index % 2]
    ).astype(jnp.int32)


def assemble_kernel(where, *refs, groups, columns):
    *sources, out_ref, extra_ref, sems = refs
    t, z, x, c = [where[n] for n in range(4)]
    half = sources[0].shape[2]
    tail = extra_ref.shape[4]
    copies = []

    def move(source, target):
        copies.append(pltpu.make_async_copy(source, target, sems.at[len(copies)]))
        copies[-1].start()

    for turn in range(2):
        for kind in range(4):
            source = sources[4 * turn + kind]
            for near in range(2):
                for ahead in range(groups):
                    far = kind % 2
                    along_t, along_x = (far, near) if kind < 2 else (near, far)
                    rows = pl.ds((kind // 2) * half, half)
                    origin = lax.rem(z + groups - ahead, groups), x ^ along_x, c ^ turn
                    side = t ^ along_t
                    start = pl.multiple_of(side * columns, 128)
                    move(
                        source.at[near, ahead, :, pl.ds(0, columns)],
                        out_ref.at[(*origin, rows, pl.ds(start, columns))],
                    )
                    if kind < 2:
                        move(
                            source.at[near, ahead, pl.ds(0, tail), pl.ds(columns, 128)],
                            extra_ref.at[(side, *origin)],
                        )
    for copy in copies:
        copy.wait()


def gather_staged(shard, vector, coords, beside_first, after):
    rows, columns = shard.shape
    groups = lax.axis_size("dp") // 4
    entries = vector.shape[0]
    tail = 16
    beside = jnp.zeros((rows * 128,), BF16).at[:entries].set(vector).reshape(rows, 128)
    shard = jnp.concatenate([shard, beside], axis=1)
    line = jnp.stack([shard] + [shift(shard, groups, by) for by in range(1, groups)])
    line, beside_first, after = lax.optimization_barrier((line, beside_first, after))
    upper, lower = line[:, : rows // 2], line[:, rows // 2 :]
    upper = jnp.stack([upper, swap(upper, "dp", 2)])
    lower = jnp.stack([lower, swap(lower, "tensor", 1)])
    mine = [upper, swap(upper, "tensor", 1), lower, swap(lower, "dp", 2)]
    theirs = [swap(piece, "dp", 1) for piece in mine]
    anywhere = pl.BlockSpec(memory_space=pl.ANY)
    inside = pl.BlockSpec(memory_space=pltpu.VMEM)
    whole, extra = pl.pallas_call(
        functools.partial(assemble_kernel, groups=groups, columns=columns),
        out_shape=(
            jax.ShapeDtypeStruct((groups, 2, 2, rows, 2 * columns), BF16),
            jax.ShapeDtypeStruct((2, groups, 2, 2, tail, 128), BF16),
        ),
        grid_spec=pltpu.PrefetchScalarGridSpec(
            num_scalar_prefetch=1,
            in_specs=[anywhere] * 8,
            out_specs=(inside, inside),
            scratch_shapes=[pltpu.SemaphoreType.DMA((24 * groups,))],
        ),
        compiler_params=pltpu.CompilerParams(vmem_limit_bytes=(4 << 20) + 16 * groups * rows * columns),
        cost_estimate=pl.CostEstimate(
            flops=0, transcendentals=0, bytes_accessed=32 * groups * rows * columns
        ),
        name="assemble",
    )(coords, *mine, *theirs)
    extra = extra.reshape(2, 4 * groups, tail * 128)[:, :, :entries]
    return whole.reshape(4 * groups * rows, 2 * columns), extra, beside_first, after


def beside_kernel(source, out_ref):
    out_ref[...] = source[0]


def beside(gathered, offset, columns):
    rows = gathered.shape[1]
    wide = min(columns, 512)
    return pl.pallas_call(
        beside_kernel,
        out_shape=jax.ShapeDtypeStruct((rows, 2 * columns), BF16),
        grid=(2, columns // wide),
        in_specs=[pl.BlockSpec((1, rows, wide), lambda t, n: (t, 0, offset // wide + n))],
        out_specs=pl.BlockSpec((rows, wide), lambda t, n: (0, t * (columns // wide) + n)),
        compiler_params=pltpu.CompilerParams(vmem_limit_bytes=(4 << 20) + 8 * rows * wide),
        cost_estimate=pl.CostEstimate(flops=0, transcendentals=0, bytes_accessed=8 * rows * columns),
        name="beside",
    )(gathered)


def take(array, index, axis):
    return lax.dynamic_index_in_dim(array, index, axis, keepdims=False)


def side(array, index):
    half = array.shape[-1] // 2
    return lax.dynamic_slice_in_dim(array, index * half, half, array.ndim - 1)


class Sum:
    def __init__(self, whole, coords, sent=BF16):
        self.t, self.z, self.x, self.c = [coords[n] for n in range(4)]
        self.groups = lax.axis_size("dp") // 4
        self.rows = whole.shape[0] // (4 * self.groups)
        self.sent = sent
        self.state = [whole.reshape(self.groups, 2, 2, self.rows, whole.shape[1])]
        self.stage = 0

    def over_tensor(self, array):
        came = swap(side(array, 1 - self.t).astype(self.sent), "tensor", 1).astype(F32)
        return (side(array, self.t).astype(F32) + came).astype(self.sent)

    def over_pair(self, array, mine, dim, step):
        came = swap(take(array, 1 - mine, dim).astype(self.sent), "dp", step).astype(F32)
        return (take(array, mine, dim).astype(F32) + came).astype(self.sent)

    def step(self):
        half = self.rows // 2
        if self.stage == 0:
            self.state = [self.over_pair(self.state[0], self.c, 2, 1)]
        elif self.stage == 1:
            whole = self.state[0]
            self.state = [
                self.over_tensor(whole[:, :, :half]),
                self.over_pair(whole[:, :, half:], self.x, 1, 2),
            ]
        elif self.stage == 2:
            upper, lower = self.state
            self.state = [self.over_pair(upper, self.x, 1, 2), self.over_tensor(lower)]
        elif self.stage == 3:
            line = jnp.concatenate(self.state, axis=1)
            total = take(line, self.z, 0).astype(F32)
            for by in range(1, self.groups):
                sent = take(line, lax.rem(self.z + by, self.groups), 0).astype(self.sent)
                total = total + shift(sent, self.groups, by).astype(F32)
            self.state = [total]
        self.stage += 1

    def result(self):
        while self.stage < 4:
            self.step()
        return self.state[0]


def advance(sums, *values):
    for one in sums:
        one.step()
    states = [one.state for one in sums]
    values, states = lax.optimization_barrier((values, states))
    for one, state in zip(sums, states):
        one.state = state
    return values if len(values) > 1 else values[0]


def to_images(rows, after=()):
    me = lax.axis_index("tensor")
    own, part = rows.shape[0] // 2, rows.shape[1]
    kept = lax.dynamic_slice_in_dim(rows, me * own, own, 0)
    sent = lax.dynamic_slice_in_dim(rows, (1 - me) * own, own, 0)
    sent, after = lax.optimization_barrier((sent, after))
    came = lax.ppermute(sent, "tensor", [(0, 1), (1, 0)])
    whole = jnp.zeros((own, 2 * part) + rows.shape[2:], rows.dtype)
    whole = lax.dynamic_update_slice_in_dim(whole, kept, me * part, 1)
    return lax.dynamic_update_slice_in_dim(whole, came, (1 - me) * part, 1), after


def split_slots(rows, slots):
    me = lax.axis_index("tensor")
    part = slots // 2
    rows = jnp.pad(rows, ((0, 0), (0, slots - rows.shape[1]), (0, 0)))
    kept = lax.dynamic_slice_in_dim(rows, me * part, part, 1)
    sent = lax.dynamic_slice_in_dim(rows, (1 - me) * part, part, 1).astype(BF16)
    return kept, sent[:, : part // 2], sent[:, part // 2 :]


def join_slots(kept, *came):
    me = lax.axis_index("tensor")
    came = jnp.concatenate(came, axis=1).astype(kept.dtype)
    first = jnp.where(me == 0, kept, came)
    second = jnp.where(me == 0, came, kept)
    return jnp.swapaxes(jnp.concatenate([first, second], axis=0), 0, 1)


def normalize(values):
    row_mean = jnp.mean(values, axis=-1, keepdims=True)
    centred = values - row_mean
    spread = jnp.mean(centred * centred, axis=-1, keepdims=True)
    inverse = lax.rsqrt(spread + epsilon)
    return centred * inverse, inverse


def normalize_back(grad, unit, inverse, gain):
    scaled = grad * gain
    mean_one = jnp.mean(scaled, axis=-1, keepdims=True)
    mean_two = jnp.mean(scaled * unit, axis=-1, keepdims=True)
    return inverse * (scaled - mean_one - unit * mean_two)


def gelu_pair(values):
    area = 0.5 * (1.0 + lax.erf(values * (0.5**0.5)))
    density = jnp.exp(-0.5 * values * values) * ((2.0 * jnp.pi) ** -0.5)
    return (values * area).astype(BF16), area + values * density


def token_sum(values):
    return jnp.sum(values.astype(F32), axis=(0, 1))


def by_images(
    inputs,
    pad_mask,
    norm1_gain,
    norm1_shift,
    qkv_weight,
    qv_bias,
    out_weight,
    out_bias,
    norm2_gain,
    norm2_shift,
    up_weight,
    up_bias,
    down_weight,
    down_bias,
    cotangent,
):
    width = inputs.shape[2]
    slots = pad_mask.shape[1]
    used = key_count(slots)
    me = lax.axis_index("tensor")
    images = inputs.shape[1] // 2
    head_width = qkv_weight.shape[2]
    pairs = head_width // PAIR
    hidden = up_weight.shape[1]
    piece = norm1_gain.shape[1]
    depth = qkv_weight.shape[0]
    coords = place()
    product = functools.partial(jnp.einsum, preferred_element_type=F32)

    x, (qkv_weight,) = to_images(jnp.swapaxes(inputs, 0, 1), (qkv_weight,))
    vector = jnp.concatenate(
        [
            v.reshape(-1)
            for v in (norm1_gain, norm1_shift, out_bias, norm2_gain, norm2_shift, down_bias, qv_bias, up_bias)
        ]
    )
    paired = jnp.swapaxes(qkv_weight.reshape(depth, 3, pairs, PAIR), 1, 2).reshape(depth, -1)
    qkv_full, flat, x, (out_weight, up_weight, down_weight) = gather_staged(
        paired, vector, coords, x, (out_weight, up_weight, down_weight)
    )
    x = x[:, :used].astype(F32)
    flat = flat.astype(F32)
    gain_one, shift_one, out_shift, gain_two, shift_two, down_shift = [
        flat[:, :, n * piece : (n + 1) * piece].reshape(width) for n in range(6)
    ]
    query_bias = flat[:, :, 6 * piece : 7 * piece].reshape(2 * pairs, PAIR)
    value_bias = flat[:, :, 7 * piece : 8 * piece].reshape(2 * pairs, PAIR)
    qkv_bias = jnp.stack([query_bias, jnp.zeros_like(query_bias), value_bias], axis=1).reshape(-1)
    up_row = flat[:, :, 8 * piece :].reshape(2 * hidden)

    others = jnp.concatenate([jnp.transpose(out_weight), up_weight], axis=1)
    others = lax.all_gather(others, ("tensor", "dp"), axis=0, tiled=True).reshape(2, width, -1)
    out_full = beside(others, 0, head_width)
    up_full = beside(others, head_width, hidden)
    last = lax.all_gather(jnp.transpose(down_weight), ("tensor", "dp"), axis=0, tiled=True)

    here = lax.dynamic_slice_in_dim(pad_mask, me * inputs.shape[0], inputs.shape[0], 1) > 0
    down_shift_grad = token_sum(cotangent * jnp.transpose(here).astype(F32)[:, :, None])
    mask = lax.dynamic_slice_in_dim(pad_mask, me * images, images, 0)
    lengths = jnp.sum(mask, axis=1).astype(jnp.int32)
    kept = (mask[:, :used] > 0).astype(F32)[:, :, None]

    unit_one, inverse_one = normalize(x)
    normed_one = (unit_one * gain_one + shift_one).astype(BF16)
    qkv = (product("bsd,dc->bsc", normed_one, qkv_full) + qkv_bias).astype(BF16)
    cotangent, qkv = lax.optimization_barrier((cotangent, qkv))
    cot = to_images(jnp.swapaxes(cotangent.astype(BF16), 0, 1))[0][:, :used].astype(F32)
    attended, lse = attention_forward(lengths, qkv)
    projected = product("bsc,dc->bsd", attended, out_full)
    after_attn = x + projected + out_shift
    unit_two, inverse_two = normalize(after_attn)
    normed_two = (unit_two * gain_two + shift_two).astype(BF16)
    up_values = product("bsd,df->bsf", normed_two, up_full) + up_row
    act, slope = gelu_pair(up_values)
    out_low = (cot * kept).astype(BF16)
    out_grad = out_low.astype(F32)

    down = Sum(product("bsd,bsf->df", out_low, act), coords)
    out_low, last, down.state = lax.optimization_barrier((out_low, last, down.state))
    down_full = beside(last.reshape(2, width, -1), 0, hidden)
    act_grad = product("bsd,df->bsf", out_low, down_full)
    up_grad = (act_grad * slope).astype(BF16)
    up_grad, normed_two = advance([down], up_grad, normed_two)
    up = Sum(product("bsd,bsf->df", normed_two, up_grad), coords)
    up_shift_grad = token_sum(up_grad)
    down.step()
    (up_grad,), (down.state, up.state) = lax.optimization_barrier(((up_grad,), (down.state, up.state)))
    normed_two_grad = product("bsf,df->bsd", up_grad, up_full)
    normed_two_grad = advance([down, up], normed_two_grad)
    gain_two_grad = token_sum(normed_two_grad * unit_two)
    shift_two_grad = token_sum(normed_two_grad)
    after_attn_grad = out_grad + normalize_back(normed_two_grad, unit_two, inverse_two, gain_two)
    out_shift_grad = token_sum(after_attn_grad)
    proj_low = after_attn_grad.astype(BF16)
    out = Sum(product("bsd,bsc->dc", proj_low, attended), coords)
    attended_grad = product("bsd,dc->bsc", proj_low, out_full).astype(BF16)
    attended_grad, act = advance([down, up], attended_grad, act)
    mlp_out = product("bsf,df->bsd", act, down_full)
    finished = (after_attn + mlp_out + down_shift) * kept
    (attended_grad, qkv), (finished, out.state) = lax.optimization_barrier(
        ((attended_grad, qkv), (finished, out.state))
    )
    qkv_grad = attention_backward(lengths, qkv, lse, attended_grad)
    held, near, far = split_slots(finished, slots)
    block_output = join_slots(held, swap(near, "tensor", 1), swap(far, "tensor", 1))
    qkv_grad, normed_one, block_output = advance([up, out], qkv_grad, normed_one, block_output)
    qkv_sum = Sum(product("bsd,bsc->dc", normed_one, qkv_grad), coords)
    qkv_grad = advance([up, out], qkv_grad)
    normed_one_grad = product("bsc,dc->bsd", qkv_grad, qkv_full)
    bias_sums = token_sum(qkv_grad).reshape(2 * pairs, 3, PAIR)
    normed_one_grad = advance([out, qkv_sum], normed_one_grad)
    gain_one_grad = token_sum(normed_one_grad * unit_one)
    shift_one_grad = token_sum(normed_one_grad)
    input_grad = after_attn_grad + normalize_back(normed_one_grad, unit_one, inverse_one, gain_one)
    input_grad, gain_one_grad, shift_one_grad = advance(
        [out, qkv_sum], input_grad, gain_one_grad, shift_one_grad
    )

    vectors = [gain_one_grad, shift_one_grad, out_shift_grad, gain_two_grad, shift_two_grad, down_shift_grad]
    vectors += [bias_sums[:, 0], bias_sums[:, 2], up_shift_grad]
    small = jnp.concatenate([v.reshape(2, lax.axis_size("dp"), -1) for v in vectors], axis=2)
    entries = small.shape[2]
    small = jnp.swapaxes(small.reshape(2, -1, entries // 2), 0, 1).reshape(-1, entries)
    small = Sum(small, coords, F32)
    held, near, far = split_slots(input_grad, slots)
    near_came = swap(near, "tensor", 1)
    near_came, far = advance([small, qkv_sum], near_came, far)
    far_came = swap(far, "tensor", 1)
    far_came, near_came = advance([small, qkv_sum], far_came, near_came)
    input_grad = join_slots(held, near_came, far_came)
    total = qkv_sum.result()
    small = small.result().reshape(1, entries)
    row = lambda n: small[:, n * piece : (n + 1) * piece]
    qkv_owned = jnp.swapaxes(total.reshape(depth, pairs, 3, PAIR), 1, 2)
    return (
        block_output,
        input_grad,
        row(0),
        row(1),
        qkv_owned.reshape(qkv_weight.shape),
        jnp.stack([row(6), row(7)], axis=0),
        jnp.transpose(out.result()),
        row(2),
        row(3),
        row(4),
        up.result(),
        small[:, 8 * piece :],
        jnp.transpose(down.result()),
        row(5),
    )


def solution(mesh):
    in_specs = (
        P("tensor", "dp", None),
        P("dp", None),
        P("tensor", "dp"),
        P("tensor", "dp"),
        P("dp", None, "tensor"),
        P(None, "tensor", "dp"),
        P("tensor", "dp"),
        P("tensor", "dp"),
        P("tensor", "dp"),
        P("tensor", "dp"),
        P("dp", "tensor"),
        P("tensor", "dp"),
        P("tensor", "dp"),
        P("tensor", "dp"),
        P("tensor", "dp", None),
    )
    out_specs = (
        P("tensor", "dp", None),
        P("tensor", "dp", None),
        P("tensor", "dp"),
        P("tensor", "dp"),
        P("dp", None, "tensor"),
        P(None, "tensor", "dp"),
        P("tensor", "dp"),
        P("tensor", "dp"),
        P("tensor", "dp"),
        P("tensor", "dp"),
        P("dp", "tensor"),
        P("tensor", "dp"),
        P("tensor", "dp"),
        P("tensor", "dp"),
    )
    dims = dict(zip(mesh.axis_names, mesh.devices.shape))

    def choose(inputs, *rest):
        whole_images = dims["tensor"] == 2 and dims["dp"] % 4 == 0 and inputs.shape[1] % 2 == 0
        return (by_images if whole_images else on_device)(inputs, *rest)

    return jax.shard_map(
        choose, mesh=mesh, in_specs=in_specs, out_specs=out_specs, check_vma=False
    )
```

```python
import functools

import jax
import jax.numpy as jnp
from jax import lax
from jax.experimental import pallas as pl
from jax.experimental.pallas import tpu as pltpu
from jax.sharding import PartitionSpec as P

HD = 64
PAIR = 2 * HD
VALID = 577
F32 = jnp.float32
BF16 = jnp.bfloat16

epsilon = 1e-06
masked_score = -1e30


def layer_norm(values, gain, shift):
    row_mean = jnp.mean(values, axis=-1, keepdims=True)
    centred = values - row_mean
    spread = jnp.mean(centred * centred, axis=-1, keepdims=True)
    return centred * lax.rsqrt(spread + epsilon) * gain + shift


def gelu_exact(values):
    return jax.nn.gelu(values, approximate=False)


def image_scores(queries, key_rows, kept_row):
    scores = jnp.einsum(
        "qhe,khe->hqk", queries, key_rows, preferred_element_type=jnp.float32
    ) * HD ** (-0.5)
    return jnp.where(kept_row[None, None, :], scores, masked_score)


def forward_image(operands):
    queries, key_rows, value_rows, kept_row = operands
    scores = image_scores(queries, key_rows, kept_row)
    row_max = jnp.max(scores, axis=-1, keepdims=True)
    exps = jnp.exp(scores - row_max)
    row_total = jnp.sum(exps, axis=-1, keepdims=True)
    soft_weights = (exps / row_total).astype(jnp.bfloat16)
    attended = jnp.einsum(
        "hqk,khe->qhe", soft_weights, value_rows, preferred_element_type=jnp.float32
    )
    return (attended.astype(jnp.bfloat16), (row_max + jnp.log(row_total))[..., 0])


def backward_image(operands):
    queries, key_rows, value_rows, kept_row, log_total, attended_grad = operands
    seq_length = queries.shape[0]
    scores = image_scores(queries, key_rows, kept_row)
    soft_float = jnp.exp(scores - log_total[..., None])
    soft_weights = soft_float.astype(jnp.bfloat16)
    value_grad = jnp.einsum(
        "hqk,qhe->khe", soft_weights, attended_grad, preferred_element_type=jnp.float32
    )
    prob_grad = jnp.einsum(
        "qhe,khe->hqk", attended_grad, value_rows, preferred_element_type=jnp.float32
    )
    score_grad = soft_float * (prob_grad - jnp.sum(prob_grad * soft_float, axis=-1, keepdims=True))
    score_grad = score_grad.astype(jnp.bfloat16)
    query_grad = jnp.einsum(
        "hqk,khe->qhe", score_grad, key_rows, preferred_element_type=jnp.float32
    ) * HD ** (-0.5)
    key_grad = jnp.einsum(
        "hqk,qhe->khe", score_grad, queries, preferred_element_type=jnp.float32
    ) * HD ** (-0.5)
    joined = jnp.concatenate(
        [
            query_grad.reshape(seq_length, -1),
            key_grad.reshape(seq_length, -1),
            value_grad.reshape(seq_length, -1),
        ],
        axis=-1,
    )
    return joined.astype(jnp.bfloat16)


def on_device(
    inputs,
    pad_mask,
    norm1_gain,
    norm1_shift,
    qkv_weight,
    qv_bias,
    out_weight,
    out_bias,
    norm2_gain,
    norm2_shift,
    up_weight,
    up_bias,
    down_weight,
    down_bias,
    cotangent,
):
    local_rows = inputs.shape[0]
    image_count = inputs.shape[1]
    model_width = inputs.shape[2]
    seq_length = pad_mask.shape[1]
    tensor_count = lax.axis_size("tensor")
    vector_stack = jnp.stack(
        [norm1_gain, norm1_shift, out_bias, norm2_gain, norm2_shift, down_bias], axis=0
    )
    gathered = (
        lax.all_gather(qkv_weight, "dp", axis=0, tiled=True),
        lax.all_gather(out_weight, "dp", axis=1, tiled=True),
        lax.all_gather(up_weight, "dp", axis=0, tiled=True),
        lax.all_gather(down_weight, "dp", axis=1, tiled=True),
        lax.all_gather(qv_bias, "dp", axis=2, tiled=True),
        lax.all_gather(up_bias, "dp", axis=1, tiled=True),
        lax.all_gather(vector_stack, "dp", axis=2, tiled=True),
    )
    qkv_full, out_full, up_full, down_full, bias_pair, bias_hidden, vector_part = gathered
    local_width = qkv_full.shape[2]
    head_count = local_width // HD
    vector_rows = (
        lax.all_gather(vector_part, "tensor", axis=1, tiled=True)
        .reshape(6, model_width)
        .astype(jnp.float32)
    )
    gain_one, shift_one, out_shift, gain_two, shift_two, down_shift = [
        vector_rows[index] for index in range(6)
    ]
    qkv_matrix = qkv_full.reshape(model_width, 3 * local_width)
    bias_row = jnp.concatenate(
        [
            bias_pair[0, 0].astype(jnp.float32),
            jnp.zeros((local_width,), jnp.float32),
            bias_pair[1, 0].astype(jnp.float32),
        ]
    )
    up_row = bias_hidden.reshape(-1).astype(jnp.float32)
    kept_all = pad_mask > 0
    first_row = lax.axis_index("tensor") * local_rows
    kept_float = jnp.transpose(lax.dynamic_slice_in_dim(kept_all, first_row, local_rows, 1)).astype(
        jnp.float32
    )[:, :, None]
    input_float = inputs.astype(jnp.float32)
    normed_one = layer_norm(input_float, gain_one, shift_one).astype(jnp.bfloat16)
    normed_all = lax.all_gather(normed_one, "tensor", axis=0, tiled=True)
    qkv_rows = (
        jnp.einsum("sbd,dc->sbc", normed_all, qkv_matrix, preferred_element_type=jnp.float32)
        + bias_row
    )
    qkv_rows = qkv_rows.astype(jnp.bfloat16)
    qkv_images = jnp.swapaxes(qkv_rows, 0, 1).reshape(image_count, seq_length, 3, head_count, HD)
    query_all = qkv_images[:, :, 0]
    key_all = qkv_images[:, :, 1]
    value_all = qkv_images[:, :, 2]
    attended_img, log_totals = lax.map(forward_image, (query_all, key_all, value_all, kept_all))
    attended_rows = jnp.swapaxes(attended_img.reshape(image_count, seq_length, local_width), 0, 1)
    row_block = attended_rows
    projected = lax.psum_scatter(
        jnp.einsum("sbc,cd->sbd", row_block, out_full, preferred_element_type=jnp.float32),
        "tensor",
        scatter_dimension=0,
        tiled=True,
    )
    after_attn = input_float + projected + out_shift
    normed_two = layer_norm(after_attn, gain_two, shift_two).astype(jnp.bfloat16)
    normed_all_two = lax.all_gather(normed_two, "tensor", axis=0, tiled=True)
    up_values = (
        jnp.einsum("sbd,df->sbf", normed_all_two, up_full, preferred_element_type=jnp.float32)
        + up_row
    )
    activated = gelu_exact(up_values).astype(jnp.bfloat16)
    row_block = activated
    mlp_out = lax.psum_scatter(
        jnp.einsum("sbf,fd->sbd", row_block, down_full, preferred_element_type=jnp.float32),
        "tensor",
        scatter_dimension=0,
        tiled=True,
    )
    block_output = (after_attn + mlp_out + down_shift) * kept_float
    qkv_back, out_back, up_back, down_back = (qkv_matrix, out_full, up_full, down_full)
    out_grad = cotangent * kept_float
    down_shift_grad = jnp.sum(out_grad, axis=(0, 1))
    out_low = out_grad.astype(jnp.bfloat16)
    out_low_all = lax.all_gather(out_low, "tensor", axis=0, tiled=True)
    down_weight_grad = jnp.einsum(
        "sbf,sbd->fd", activated, out_low_all, preferred_element_type=jnp.float32
    )
    act_grad = jnp.einsum("sbd,fd->sbf", out_low_all, down_back, preferred_element_type=jnp.float32)
    _, gelu_back = jax.vjp(gelu_exact, up_values)
    up_grad = gelu_back(act_grad)[0].astype(jnp.bfloat16)
    up_shift_grad = jnp.sum(up_grad.astype(jnp.float32), axis=(0, 1))
    up_weight_grad = jnp.einsum(
        "sbd,sbf->df", normed_all_two, up_grad, preferred_element_type=jnp.float32
    )
    row_block = up_grad
    normed_two_grad = lax.psum_scatter(
        jnp.einsum("sbf,df->sbd", row_block, up_back, preferred_element_type=jnp.float32),
        "tensor",
        scatter_dimension=0,
        tiled=True,
    )
    _, norm_two_back = jax.vjp(layer_norm, after_attn, gain_two, shift_two)
    attn_side, gain_two_grad, shift_two_grad = norm_two_back(normed_two_grad)
    after_attn_grad = out_grad + attn_side
    out_shift_grad = jnp.sum(after_attn_grad, axis=(0, 1))
    proj_low = after_attn_grad.astype(jnp.bfloat16)
    proj_low_all = lax.all_gather(proj_low, "tensor", axis=0, tiled=True)
    out_weight_grad = jnp.einsum(
        "sbc,sbd->cd", attended_rows, proj_low_all, preferred_element_type=jnp.float32
    )
    attended_grad = jnp.einsum(
        "sbd,cd->sbc", proj_low_all, out_back, preferred_element_type=jnp.float32
    )
    attended_grad = attended_grad.astype(jnp.bfloat16)
    attended_grad_img = jnp.swapaxes(attended_grad, 0, 1).reshape(
        image_count, seq_length, head_count, HD
    )
    qkv_grad_img = lax.map(
        backward_image, (query_all, key_all, value_all, kept_all, log_totals, attended_grad_img)
    )
    qkv_grad = jnp.swapaxes(qkv_grad_img, 0, 1)
    qkv_sums = jnp.sum(qkv_grad.astype(jnp.float32), axis=(0, 1))
    qv_grad = jnp.stack([qkv_sums[:local_width], qkv_sums[2 * local_width :]], axis=0).reshape(
        2, 1, local_width
    )
    qkv_weight_grad = jnp.einsum(
        "sbd,sbc->dc", normed_all, qkv_grad, preferred_element_type=jnp.float32
    )
    qkv_weight_grad = qkv_weight_grad.reshape(model_width, 3, local_width)
    row_block = qkv_grad
    normed_one_grad = lax.psum_scatter(
        jnp.einsum("sbc,dc->sbd", row_block, qkv_back, preferred_element_type=jnp.float32),
        "tensor",
        scatter_dimension=0,
        tiled=True,
    )
    _, norm_one_back = jax.vjp(layer_norm, input_float, gain_one, shift_one)
    input_side, gain_one_grad, shift_one_grad = norm_one_back(normed_one_grad)
    input_grad = after_attn_grad + input_side
    vector_grads = jnp.stack(
        [
            gain_one_grad,
            shift_one_grad,
            out_shift_grad,
            gain_two_grad,
            shift_two_grad,
            down_shift_grad,
        ],
        axis=0,
    ).reshape(6, tensor_count, model_width // tensor_count)
    vector_local = lax.psum_scatter(vector_grads, "tensor", scatter_dimension=1, tiled=True)
    owned = (
        lax.psum_scatter(qkv_weight_grad, "dp", scatter_dimension=0, tiled=True),
        lax.psum_scatter(out_weight_grad, "dp", scatter_dimension=1, tiled=True),
        lax.psum_scatter(up_weight_grad, "dp", scatter_dimension=0, tiled=True),
        lax.psum_scatter(down_weight_grad, "dp", scatter_dimension=1, tiled=True),
        lax.psum_scatter(qv_grad, "dp", scatter_dimension=2, tiled=True),
        lax.psum_scatter(up_shift_grad.reshape(1, -1), "dp", scatter_dimension=1, tiled=True),
        lax.psum_scatter(vector_local, "dp", scatter_dimension=2, tiled=True),
    )
    qkv_owned, out_owned, up_owned, down_owned, qv_owned, hidden_owned, vector_owned = owned
    return (
        block_output,
        input_grad,
        vector_owned[0],
        vector_owned[1],
        qkv_owned,
        qv_owned,
        out_owned,
        vector_owned[2],
        vector_owned[3],
        vector_owned[4],
        up_owned,
        hidden_owned,
        down_owned,
        vector_owned[5],
    )


NT = (((1,), (1,)), ((), ()))
NN = (((1,), (0,)), ((), ()))


def dot_nn(a, b):
    return lax.dot_general(a, b, NN, preferred_element_type=F32)


def dot_nt(a, b):
    return lax.dot_general(a, b, NT, preferred_element_type=F32)


def attention_forward_kernel(lengths, q_ref, k_ref, v_ref, o_ref, lse_ref, *, key_rows):
    length = lengths[pl.program_id(0)]
    queries = q_ref[0] * jnp.asarray(HD**-0.5, BF16)
    keys = k_ref[0, :key_rows]
    values_t = jnp.transpose(v_ref[0, :key_rows].astype(F32)).astype(BF16)
    lane = lax.broadcasted_iota(jnp.int32, (key_rows, PAIR), 1)
    valid = lax.broadcasted_iota(jnp.int32, (key_rows, q_ref.shape[1]), 0) < length
    outs = []
    for head in range(2):
        own = (lane >= head * HD) & (lane < (head + 1) * HD)
        scores = dot_nt(jnp.where(own, keys, jnp.zeros_like(keys)), queries)
        scores = jnp.where(valid, scores, masked_score)
        top = jnp.max(scores, axis=0, keepdims=True)
        exps = jnp.exp(scores - top)
        total = jnp.sum(exps, axis=0, keepdims=True)
        lse_ref[0, 0, head : head + 1, :] = top + jnp.log(total)
        probs = (exps * (1.0 / total)).astype(BF16)
        outs.append(dot_nn(values_t[head * HD : (head + 1) * HD], probs))
    o_ref[0] = jnp.transpose(jnp.concatenate(outs, axis=0)).astype(BF16)


def attention_backward_kernel(
    lengths, q_ref, k_ref, v_ref, lse_ref, g_ref, d_ref, *, key_rows
):
    length = lengths[pl.program_id(0)]
    slots = q_ref.shape[1]
    scale = HD**-0.5
    plain = q_ref[0]
    queries = plain * jnp.asarray(scale, BF16)
    keys = k_ref[0, :key_rows]
    values = v_ref[0, :key_rows]
    grads = g_ref[0]
    keys_t = jnp.transpose(keys.astype(F32)).astype(BF16)
    lane = lax.broadcasted_iota(jnp.int32, (key_rows, PAIR), 1)
    valid = lax.broadcasted_iota(jnp.int32, (key_rows, slots), 0) < length
    zero = jnp.zeros_like(keys)
    dqs, dks, dvs = [], [], []
    for head in range(2):
        own = (lane >= head * HD) & (lane < (head + 1) * HD)
        scores = dot_nt(jnp.where(own, keys, zero), queries)
        soft = jnp.where(valid, jnp.exp(scores - lse_ref[0, 0, head : head + 1, :]), 0.0)
        prob_grad = dot_nt(jnp.where(own, values, zero), grads)
        inner = jnp.sum(prob_grad * soft, axis=0, keepdims=True)
        score_grad = (soft * (prob_grad - inner)).astype(BF16)
        dvs.append(dot_nn(soft.astype(BF16), grads))
        dks.append(dot_nn(score_grad, plain))
        dqs.append(dot_nn(keys_t[head * HD : (head + 1) * HD], score_grad))
    first = lane < HD
    d_ref[0, :, :PAIR] = (jnp.transpose(jnp.concatenate(dqs, axis=0)) * scale).astype(BF16)
    d_ref[0, :key_rows, PAIR : 2 * PAIR] = (jnp.where(first, dks[0], dks[1]) * scale).astype(BF16)
    d_ref[0, :key_rows, 2 * PAIR :] = jnp.where(first, dvs[0], dvs[1]).astype(BF16)
    if key_rows < slots:
        d_ref[0, key_rows:, PAIR:] = jnp.zeros((slots - key_rows, 2 * PAIR), BF16)


def key_count(slots):
    return min(slots, -(-VALID // 16) * 16)


def pair_block(slots, each, offset):
    return pl.BlockSpec((1, slots, PAIR), lambda b, p, ln: (b, 0, each * p + offset))


def attention_forward(lengths, qkv):
    images, slots, columns = qkv.shape
    width = columns // 3
    pairs = width // PAIR
    return pl.pallas_call(
        functools.partial(attention_forward_kernel, key_rows=key_count(slots)),
        out_shape=(
            jax.ShapeDtypeStruct((images, slots, width), BF16),
            jax.ShapeDtypeStruct((images, pairs, 2, slots), F32),
        ),
        grid_spec=pltpu.PrefetchScalarGridSpec(
            num_scalar_prefetch=1,
            grid=(images, pairs),
            in_specs=[pair_block(slots, 3, n) for n in range(3)],
            out_specs=(
                pair_block(slots, 1, 0),
                pl.BlockSpec((1, 1, 2, slots), lambda b, p, ln: (b, p, 0, 0)),
            ),
        ),
        compiler_params=pltpu.CompilerParams(vmem_limit_bytes=40 << 20),
        cost_estimate=pl.CostEstimate(
            flops=images * pairs * 2 * 4 * slots * slots * PAIR,
            bytes_accessed=images * slots * width * 8,
            transcendentals=images * pairs * 2 * slots * slots,
        ),
        name="attention_forward",
    )(lengths, qkv, qkv, qkv)


def attention_backward(lengths, qkv, lse, grads):
    images, slots, columns = qkv.shape
    width = columns // 3
    pairs = width // PAIR
    return pl.pallas_call(
        functools.partial(attention_backward_kernel, key_rows=key_count(slots)),
        out_shape=jax.ShapeDtypeStruct(qkv.shape, BF16),
        grid_spec=pltpu.PrefetchScalarGridSpec(
            num_scalar_prefetch=1,
            grid=(images, pairs),
            in_specs=[pair_block(slots, 3, n) for n in range(3)]
            + [
                pl.BlockSpec((1, 1, 2, slots), lambda b, p, ln: (b, p, 0, 0)),
                pair_block(slots, 1, 0),
            ],
            out_specs=pl.BlockSpec((1, slots, 3 * PAIR), lambda b, p, ln: (b, 0, p)),
        ),
        compiler_params=pltpu.CompilerParams(vmem_limit_bytes=40 << 20),
        cost_estimate=pl.CostEstimate(
            flops=images * pairs * 2 * 10 * slots * slots * PAIR,
            bytes_accessed=images * slots * width * 14,
            transcendentals=images * pairs * 2 * slots * slots,
        ),
        name="attention_backward",
    )(lengths, qkv, qkv, qkv, lse, grads)


def swap(array, axis, step):
    return lax.ppermute(array, axis, [(n, n ^ step) for n in range(lax.axis_size(axis))])


def shift(array, groups, by):
    count = 4 * groups
    return lax.ppermute(array, "dp", [(n, (n + 4 * by) % count) for n in range(count)])


def place():
    index = lax.axis_index("dp")
    return jnp.stack(
        [lax.axis_index("tensor"), index // 4, (index // 2) % 2, index % 2]
    ).astype(jnp.int32)


def assemble_kernel(where, *refs, groups, columns):
    *sources, out_ref, extra_ref, sems = refs
    t, z, x, c = [where[n] for n in range(4)]
    half = sources[0].shape[2]
    tail = extra_ref.shape[4]
    copies = []

    def move(source, target):
        copies.append(pltpu.make_async_copy(source, target, sems.at[len(copies)]))
        copies[-1].start()

    for turn in range(2):
        for kind in range(4):
            source = sources[4 * turn + kind]
            for near in range(2):
                for ahead in range(groups):
                    far = kind % 2
                    along_t, along_x = (far, near) if kind < 2 else (near, far)
                    rows = pl.ds((kind // 2) * half, half)
                    origin = lax.rem(z + groups - ahead, groups), x ^ along_x, c ^ turn
                    side = t ^ along_t
                    start = pl.multiple_of(side * columns, 128)
                    move(
                        source.at[near, ahead, :, pl.ds(0, columns)],
                        out_ref.at[(*origin, rows, pl.ds(start, columns))],
                    )
                    if kind < 2:
                        move(
                            source.at[near, ahead, pl.ds(0, tail), pl.ds(columns, 128)],
                            extra_ref.at[(side, *origin)],
                        )
    for copy in copies:
        copy.wait()


def gather_staged(shard, vector, coords, beside_first, after):
    rows, columns = shard.shape
    groups = lax.axis_size("dp") // 4
    entries = vector.shape[0]
    tail = 16
    beside = jnp.zeros((rows * 128,), BF16).at[:entries].set(vector).reshape(rows, 128)
    shard = jnp.concatenate([shard, beside], axis=1)
    line = jnp.stack([shard] + [shift(shard, groups, by) for by in range(1, groups)])
    line, beside_first, after = lax.optimization_barrier((line, beside_first, after))
    upper, lower = line[:, : rows // 2], line[:, rows // 2 :]
    upper = jnp.stack([upper, swap(upper, "dp", 2)])
    lower = jnp.stack([lower, swap(lower, "tensor", 1)])
    mine = [upper, swap(upper, "tensor", 1), lower, swap(lower, "dp", 2)]
    theirs = [swap(piece, "dp", 1) for piece in mine]
    anywhere = pl.BlockSpec(memory_space=pl.ANY)
    inside = pl.BlockSpec(memory_space=pltpu.VMEM)
    whole, extra = pl.pallas_call(
        functools.partial(assemble_kernel, groups=groups, columns=columns),
        out_shape=(
            jax.ShapeDtypeStruct((groups, 2, 2, rows, 2 * columns), BF16),
            jax.ShapeDtypeStruct((2, groups, 2, 2, tail, 128), BF16),
        ),
        grid_spec=pltpu.PrefetchScalarGridSpec(
            num_scalar_prefetch=1,
            in_specs=[anywhere] * 8,
            out_specs=(inside, inside),
            scratch_shapes=[pltpu.SemaphoreType.DMA((24 * groups,))],
        ),
        compiler_params=pltpu.CompilerParams(vmem_limit_bytes=(4 << 20) + 16 * groups * rows * columns),
        cost_estimate=pl.CostEstimate(
            flops=0, transcendentals=0, bytes_accessed=32 * groups * rows * columns
        ),
        name="assemble",
    )(coords, *mine, *theirs)
    extra = extra.reshape(2, 4 * groups, tail * 128)[:, :, :entries]
    return whole.reshape(4 * groups * rows, 2 * columns), extra, beside_first, after


def beside_kernel(source, out_ref):
    out_ref[...] = source[0]


def beside(gathered, offset, columns):
    rows = gathered.shape[1]
    wide = min(columns, 512)
    return pl.pallas_call(
        beside_kernel,
        out_shape=jax.ShapeDtypeStruct((rows, 2 * columns), BF16),
        grid=(2, columns // wide),
        in_specs=[pl.BlockSpec((1, rows, wide), lambda t, n: (t, 0, offset // wide + n))],
        out_specs=pl.BlockSpec((rows, wide), lambda t, n: (0, t * (columns // wide) + n)),
        compiler_params=pltpu.CompilerParams(vmem_limit_bytes=(4 << 20) + 8 * rows * wide),
        cost_estimate=pl.CostEstimate(flops=0, transcendentals=0, bytes_accessed=8 * rows * columns),
        name="beside",
    )(gathered)


def take(array, index, axis):
    return lax.dynamic_index_in_dim(array, index, axis, keepdims=False)


def side(array, index):
    half = array.shape[-1] // 2
    return lax.dynamic_slice_in_dim(array, index * half, half, array.ndim - 1)


class Sum:
    def __init__(self, whole, coords, sent=BF16):
        self.t, self.z, self.x, self.c = [coords[n] for n in range(4)]
        self.groups = lax.axis_size("dp") // 4
        self.rows = whole.shape[0] // (4 * self.groups)
        self.sent = sent
        self.state = [whole.reshape(self.groups, 2, 2, self.rows, whole.shape[1])]
        self.stage = 0

    def over_tensor(self, array):
        came = swap(side(array, 1 - self.t).astype(self.sent), "tensor", 1).astype(F32)
        return (side(array, self.t).astype(F32) + came).astype(self.sent)

    def over_pair(self, array, mine, dim, step):
        came = swap(take(array, 1 - mine, dim).astype(self.sent), "dp", step).astype(F32)
        return (take(array, mine, dim).astype(F32) + came).astype(self.sent)

    def step(self):
        half = self.rows // 2
        if self.stage == 0:
            self.state = [self.over_pair(self.state[0], self.c, 2, 1)]
        elif self.stage == 1:
            whole = self.state[0]
            self.state = [
                self.over_tensor(whole[:, :, :half]),
                self.over_pair(whole[:, :, half:], self.x, 1, 2),
            ]
        elif self.stage == 2:
            upper, lower = self.state
            self.state = [self.over_pair(upper, self.x, 1, 2), self.over_tensor(lower)]
        elif self.stage == 3:
            line = jnp.concatenate(self.state, axis=1)
            total = take(line, self.z, 0).astype(F32)
            for by in range(1, self.groups):
                sent = take(line, lax.rem(self.z + by, self.groups), 0).astype(self.sent)
                total = total + shift(sent, self.groups, by).astype(F32)
            self.state = [total]
        self.stage += 1

    def result(self):
        while self.stage < 4:
            self.step()
        return self.state[0]


def advance(sums, *values):
    for one in sums:
        one.step()
    states = [one.state for one in sums]
    values, states = lax.optimization_barrier((values, states))
    for one, state in zip(sums, states):
        one.state = state
    return values if len(values) > 1 else values[0]


def to_images(rows, after=()):
    me = lax.axis_index("tensor")
    own, part = rows.shape[0] // 2, rows.shape[1]
    kept = lax.dynamic_slice_in_dim(rows, me * own, own, 0)
    sent = lax.dynamic_slice_in_dim(rows, (1 - me) * own, own, 0)
    sent, after = lax.optimization_barrier((sent, after))
    came = lax.ppermute(sent, "tensor", [(0, 1), (1, 0)])
    whole = jnp.zeros((own, 2 * part) + rows.shape[2:], rows.dtype)
    whole = lax.dynamic_update_slice_in_dim(whole, kept, me * part, 1)
    return lax.dynamic_update_slice_in_dim(whole, came, (1 - me) * part, 1), after


def split_slots(rows, slots):
    me = lax.axis_index("tensor")
    part = slots // 2
    rows = jnp.pad(rows, ((0, 0), (0, slots - rows.shape[1]), (0, 0)))
    kept = lax.dynamic_slice_in_dim(rows, me * part, part, 1)
    sent = lax.dynamic_slice_in_dim(rows, (1 - me) * part, part, 1).astype(BF16)
    return kept, sent[:, : part // 2], sent[:, part // 2 :]


def join_slots(kept, *came):
    me = lax.axis_index("tensor")
    came = jnp.concatenate(came, axis=1).astype(kept.dtype)
    first = jnp.where(me == 0, kept, came)
    second = jnp.where(me == 0, came, kept)
    return jnp.swapaxes(jnp.concatenate([first, second], axis=0), 0, 1)


def normalize(values):
    row_mean = jnp.mean(values, axis=-1, keepdims=True)
    centred = values - row_mean
    spread = jnp.mean(centred * centred, axis=-1, keepdims=True)
    inverse = lax.rsqrt(spread + epsilon)
    return centred * inverse, inverse


def normalize_back(grad, unit, inverse, gain):
    scaled = grad * gain
    mean_one = jnp.mean(scaled, axis=-1, keepdims=True)
    mean_two = jnp.mean(scaled * unit, axis=-1, keepdims=True)
    return inverse * (scaled - mean_one - unit * mean_two)


def gelu_pair(values):
    area = 0.5 * (1.0 + lax.erf(values * (0.5**0.5)))
    density = jnp.exp(-0.5 * values * values) * ((2.0 * jnp.pi) ** -0.5)
    return (values * area).astype(BF16), area + values * density


def token_sum(values):
    return jnp.sum(values.astype(F32), axis=(0, 1))


def by_images(
    inputs,
    pad_mask,
    norm1_gain,
    norm1_shift,
    qkv_weight,
    qv_bias,
    out_weight,
    out_bias,
    norm2_gain,
    norm2_shift,
    up_weight,
    up_bias,
    down_weight,
    down_bias,
    cotangent,
):
    width = inputs.shape[2]
    slots = pad_mask.shape[1]
    used = key_count(slots)
    me = lax.axis_index("tensor")
    images = inputs.shape[1] // 2
    head_width = qkv_weight.shape[2]
    pairs = head_width // PAIR
    hidden = up_weight.shape[1]
    piece = norm1_gain.shape[1]
    depth = qkv_weight.shape[0]
    coords = place()
    product = functools.partial(jnp.einsum, preferred_element_type=F32)

    x, (qkv_weight,) = to_images(jnp.swapaxes(inputs, 0, 1), (qkv_weight,))
    vector = jnp.concatenate(
        [
            v.reshape(-1)
            for v in (norm1_gain, norm1_shift, out_bias, norm2_gain, norm2_shift, down_bias, qv_bias, up_bias)
        ]
    )
    paired = jnp.swapaxes(qkv_weight.reshape(depth, 3, pairs, PAIR), 1, 2).reshape(depth, -1)
    qkv_full, flat, x, (out_weight, up_weight, down_weight) = gather_staged(
        paired, vector, coords, x, (out_weight, up_weight, down_weight)
    )
    x = x[:, :used].astype(F32)
    flat = flat.astype(F32)
    gain_one, shift_one, out_shift, gain_two, shift_two, down_shift = [
        flat[:, :, n * piece : (n + 1) * piece].reshape(width) for n in range(6)
    ]
    query_bias = flat[:, :, 6 * piece : 7 * piece].reshape(2 * pairs, PAIR)
    value_bias = flat[:, :, 7 * piece : 8 * piece].reshape(2 * pairs, PAIR)
    qkv_bias = jnp.stack([query_bias, jnp.zeros_like(query_bias), value_bias], axis=1).reshape(-1)
    up_row = flat[:, :, 8 * piece :].reshape(2 * hidden)

    others = jnp.concatenate([jnp.transpose(out_weight), up_weight], axis=1)
    others = lax.all_gather(others, ("tensor", "dp"), axis=0, tiled=True).reshape(2, width, -1)
    out_full = beside(others, 0, head_width)
    up_full = beside(others, head_width, hidden)
    last = lax.all_gather(jnp.transpose(down_weight), ("tensor", "dp"), axis=0, tiled=True)

    here = lax.dynamic_slice_in_dim(pad_mask, me * inputs.shape[0], inputs.shape[0], 1) > 0
    down_shift_grad = token_sum(cotangent * jnp.transpose(here).astype(F32)[:, :, None])
    mask = lax.dynamic_slice_in_dim(pad_mask, me * images, images, 0)
    lengths = jnp.sum(mask, axis=1).astype(jnp.int32)
    kept = (mask[:, :used] > 0).astype(F32)[:, :, None]

    unit_one, inverse_one = normalize(x)
    normed_one = (unit_one * gain_one + shift_one).astype(BF16)
    qkv = (product("bsd,dc->bsc", normed_one, qkv_full) + qkv_bias).astype(BF16)
    cotangent, qkv = lax.optimization_barrier((cotangent, qkv))
    cot = to_images(jnp.swapaxes(cotangent.astype(BF16), 0, 1))[0][:, :used].astype(F32)
    attended, lse = attention_forward(lengths, qkv)
    projected = product("bsc,dc->bsd", attended, out_full)
    after_attn = x + projected + out_shift
    unit_two, inverse_two = normalize(after_attn)
    normed_two = (unit_two * gain_two + shift_two).astype(BF16)
    up_values = product("bsd,df->bsf", normed_two, up_full) + up_row
    act, slope = gelu_pair(up_values)
    out_low = (cot * kept).astype(BF16)
    out_grad = out_low.astype(F32)

    down = Sum(product("bsd,bsf->df", out_low, act), coords)
    out_low, last, down.state = lax.optimization_barrier((out_low, last, down.state))
    down_full = beside(last.reshape(2, width, -1), 0, hidden)
    act_grad = product("bsd,df->bsf", out_low, down_full)
    up_grad = (act_grad * slope).astype(BF16)
    up = Sum(product("bsd,bsf->df", normed_two, up_grad), coords)
    up_shift_grad = token_sum(up_grad)
    down.step()
    up_grad, down.state, up.state = lax.optimization_barrier((up_grad, down.state, up.state))
    normed_two_grad = product("bsf,df->bsd", up_grad, up_full)
    normed_two_grad = advance([down, up], normed_two_grad)
    gain_two_grad = token_sum(normed_two_grad * unit_two)
    shift_two_grad = token_sum(normed_two_grad)
    after_attn_grad = out_grad + normalize_back(normed_two_grad, unit_two, inverse_two, gain_two)
    out_shift_grad = token_sum(after_attn_grad)
    proj_low = after_attn_grad.astype(BF16)
    out = Sum(product("bsd,bsc->dc", proj_low, attended), coords)
    attended_grad = product("bsd,dc->bsc", proj_low, out_full).astype(BF16)
    attended_grad, act = advance([down], attended_grad, act)
    mlp_out = product("bsf,df->bsd", act, down_full)
    finished = (after_attn + mlp_out + down_shift) * kept
    down.step()
    up.step()
    attended_grad, qkv, finished, out.state, down.state, up.state = lax.optimization_barrier(
        (attended_grad, qkv, finished, out.state, down.state, up.state)
    )
    qkv_grad = attention_backward(lengths, qkv, lse, attended_grad)
    held, near, far = split_slots(finished, slots)
    block_output = join_slots(held, swap(near, "tensor", 1), swap(far, "tensor", 1))
    qkv_grad, normed_one, block_output = advance([up, out], qkv_grad, normed_one, block_output)
    qkv_sum = Sum(product("bsd,bsc->dc", normed_one, qkv_grad), coords)
    qkv_grad = advance([up, out], qkv_grad)
    normed_one_grad = product("bsc,dc->bsd", qkv_grad, qkv_full)
    bias_sums = token_sum(qkv_grad).reshape(2 * pairs, 3, PAIR)
    normed_one_grad = advance([out, qkv_sum], normed_one_grad)
    gain_one_grad = token_sum(normed_one_grad * unit_one)
    shift_one_grad = token_sum(normed_one_grad)
    input_grad = after_attn_grad + normalize_back(normed_one_grad, unit_one, inverse_one, gain_one)
    input_grad, gain_one_grad, shift_one_grad = advance(
        [out, qkv_sum], input_grad, gain_one_grad, shift_one_grad
    )

    vectors = [gain_one_grad, shift_one_grad, out_shift_grad, gain_two_grad, shift_two_grad, down_shift_grad]
    vectors += [bias_sums[:, 0], bias_sums[:, 2], up_shift_grad]
    small = jnp.concatenate([v.reshape(2, lax.axis_size("dp"), -1) for v in vectors], axis=2)
    entries = small.shape[2]
    small = jnp.swapaxes(small.reshape(2, -1, entries // 2), 0, 1).reshape(-1, entries)
    small = Sum(small, coords, F32)
    held, near, far = split_slots(input_grad, slots)
    near_came = swap(near, "tensor", 1)
    near_came, far = advance([small, qkv_sum], near_came, far)
    far_came = swap(far, "tensor", 1)
    far_came, near_came = advance([small, qkv_sum], far_came, near_came)
    input_grad = join_slots(held, near_came, far_came)
    total = qkv_sum.result()
    small = small.result().reshape(1, entries)
    row = lambda n: small[:, n * piece : (n + 1) * piece]
    qkv_owned = jnp.swapaxes(total.reshape(depth, pairs, 3, PAIR), 1, 2)
    return (
        block_output,
        input_grad,
        row(0),
        row(1),
        qkv_owned.reshape(qkv_weight.shape),
        jnp.stack([row(6), row(7)], axis=0),
        jnp.transpose(out.result()),
        row(2),
        row(3),
        row(4),
        up.result(),
        small[:, 8 * piece :],
        jnp.transpose(down.result()),
        row(5),
    )


def solution(mesh):
    in_specs = (
        P("tensor", "dp", None),
        P("dp", None),
        P("tensor", "dp"),
        P("tensor", "dp"),
        P("dp", None, "tensor"),
        P(None, "tensor", "dp"),
        P("tensor", "dp"),
        P("tensor", "dp"),
        P("tensor", "dp"),
        P("tensor", "dp"),
        P("dp", "tensor"),
        P("tensor", "dp"),
        P("tensor", "dp"),
        P("tensor", "dp"),
        P("tensor", "dp", None),
    )
    out_specs = (
        P("tensor", "dp", None),
        P("tensor", "dp", None),
        P("tensor", "dp"),
        P("tensor", "dp"),
        P("dp", None, "tensor"),
        P(None, "tensor", "dp"),
        P("tensor", "dp"),
        P("tensor", "dp"),
        P("tensor", "dp"),
        P("tensor", "dp"),
        P("dp", "tensor"),
        P("tensor", "dp"),
        P("tensor", "dp"),
        P("tensor", "dp"),
    )
    dims = dict(zip(mesh.axis_names, mesh.devices.shape))

    def choose(inputs, *rest):
        whole_images = dims["tensor"] == 2 and dims["dp"] % 4 == 0 and inputs.shape[1] % 2 == 0
        return (by_images if whole_images else on_device)(inputs, *rest)

    return jax.shard_map(
        choose, mesh=mesh, in_specs=in_specs, out_specs=out_specs, check_vma=False
    )
```

```python
import functools

import jax
import jax.numpy as jnp
from jax import lax
from jax.experimental import pallas as pl
from jax.experimental.pallas import tpu as pltpu
from jax.sharding import PartitionSpec as P

HD = 64
PAIR = 2 * HD
VALID = 577
SURE = 288
F32 = jnp.float32
BF16 = jnp.bfloat16

epsilon = 1e-06
masked_score = -1e30


def layer_norm(values, gain, shift):
    row_mean = jnp.mean(values, axis=-1, keepdims=True)
    centred = values - row_mean
    spread = jnp.mean(centred * centred, axis=-1, keepdims=True)
    return centred * lax.rsqrt(spread + epsilon) * gain + shift


def gelu_exact(values):
    return jax.nn.gelu(values, approximate=False)


def image_scores(queries, key_rows, kept_row):
    scores = jnp.einsum(
        "qhe,khe->hqk", queries, key_rows, preferred_element_type=jnp.float32
    ) * HD ** (-0.5)
    return jnp.where(kept_row[None, None, :], scores, masked_score)


def forward_image(operands):
    queries, key_rows, value_rows, kept_row = operands
    scores = image_scores(queries, key_rows, kept_row)
    row_max = jnp.max(scores, axis=-1, keepdims=True)
    exps = jnp.exp(scores - row_max)
    row_total = jnp.sum(exps, axis=-1, keepdims=True)
    soft_weights = (exps / row_total).astype(jnp.bfloat16)
    attended = jnp.einsum(
        "hqk,khe->qhe", soft_weights, value_rows, preferred_element_type=jnp.float32
    )
    return (attended.astype(jnp.bfloat16), (row_max + jnp.log(row_total))[..., 0])


def backward_image(operands):
    queries, key_rows, value_rows, kept_row, log_total, attended_grad = operands
    seq_length = queries.shape[0]
    scores = image_scores(queries, key_rows, kept_row)
    soft_float = jnp.exp(scores - log_total[..., None])
    soft_weights = soft_float.astype(jnp.bfloat16)
    value_grad = jnp.einsum(
        "hqk,qhe->khe", soft_weights, attended_grad, preferred_element_type=jnp.float32
    )
    prob_grad = jnp.einsum(
        "qhe,khe->hqk", attended_grad, value_rows, preferred_element_type=jnp.float32
    )
    score_grad = soft_float * (prob_grad - jnp.sum(prob_grad * soft_float, axis=-1, keepdims=True))
    score_grad = score_grad.astype(jnp.bfloat16)
    query_grad = jnp.einsum(
        "hqk,khe->qhe", score_grad, key_rows, preferred_element_type=jnp.float32
    ) * HD ** (-0.5)
    key_grad = jnp.einsum(
        "hqk,qhe->khe", score_grad, queries, preferred_element_type=jnp.float32
    ) * HD ** (-0.5)
    joined = jnp.concatenate(
        [
            query_grad.reshape(seq_length, -1),
            key_grad.reshape(seq_length, -1),
            value_grad.reshape(seq_length, -1),
        ],
        axis=-1,
    )
    return joined.astype(jnp.bfloat16)


def on_device(
    inputs,
    pad_mask,
    norm1_gain,
    norm1_shift,
    qkv_weight,
    qv_bias,
    out_weight,
    out_bias,
    norm2_gain,
    norm2_shift,
    up_weight,
    up_bias,
    down_weight,
    down_bias,
    cotangent,
):
    local_rows = inputs.shape[0]
    image_count = inputs.shape[1]
    model_width = inputs.shape[2]
    seq_length = pad_mask.shape[1]
    tensor_count = lax.axis_size("tensor")
    vector_stack = jnp.stack(
        [norm1_gain, norm1_shift, out_bias, norm2_gain, norm2_shift, down_bias], axis=0
    )
    gathered = (
        lax.all_gather(qkv_weight, "dp", axis=0, tiled=True),
        lax.all_gather(out_weight, "dp", axis=1, tiled=True),
        lax.all_gather(up_weight, "dp", axis=0, tiled=True),
        lax.all_gather(down_weight, "dp", axis=1, tiled=True),
        lax.all_gather(qv_bias, "dp", axis=2, tiled=True),
        lax.all_gather(up_bias, "dp", axis=1, tiled=True),
        lax.all_gather(vector_stack, "dp", axis=2, tiled=True),
    )
    qkv_full, out_full, up_full, down_full, bias_pair, bias_hidden, vector_part = gathered
    local_width = qkv_full.shape[2]
    head_count = local_width // HD
    vector_rows = (
        lax.all_gather(vector_part, "tensor", axis=1, tiled=True)
        .reshape(6, model_width)
        .astype(jnp.float32)
    )
    gain_one, shift_one, out_shift, gain_two, shift_two, down_shift = [
        vector_rows[index] for index in range(6)
    ]
    qkv_matrix = qkv_full.reshape(model_width, 3 * local_width)
    bias_row = jnp.concatenate(
        [
            bias_pair[0, 0].astype(jnp.float32),
            jnp.zeros((local_width,), jnp.float32),
            bias_pair[1, 0].astype(jnp.float32),
        ]
    )
    up_row = bias_hidden.reshape(-1).astype(jnp.float32)
    kept_all = pad_mask > 0
    first_row = lax.axis_index("tensor") * local_rows
    kept_float = jnp.transpose(lax.dynamic_slice_in_dim(kept_all, first_row, local_rows, 1)).astype(
        jnp.float32
    )[:, :, None]
    input_float = inputs.astype(jnp.float32)
    normed_one = layer_norm(input_float, gain_one, shift_one).astype(jnp.bfloat16)
    normed_all = lax.all_gather(normed_one, "tensor", axis=0, tiled=True)
    qkv_rows = (
        jnp.einsum("sbd,dc->sbc", normed_all, qkv_matrix, preferred_element_type=jnp.float32)
        + bias_row
    )
    qkv_rows = qkv_rows.astype(jnp.bfloat16)
    qkv_images = jnp.swapaxes(qkv_rows, 0, 1).reshape(image_count, seq_length, 3, head_count, HD)
    query_all = qkv_images[:, :, 0]
    key_all = qkv_images[:, :, 1]
    value_all = qkv_images[:, :, 2]
    attended_img, log_totals = lax.map(forward_image, (query_all, key_all, value_all, kept_all))
    attended_rows = jnp.swapaxes(attended_img.reshape(image_count, seq_length, local_width), 0, 1)
    row_block = attended_rows
    projected = lax.psum_scatter(
        jnp.einsum("sbc,cd->sbd", row_block, out_full, preferred_element_type=jnp.float32),
        "tensor",
        scatter_dimension=0,
        tiled=True,
    )
    after_attn = input_float + projected + out_shift
    normed_two = layer_norm(after_attn, gain_two, shift_two).astype(jnp.bfloat16)
    normed_all_two = lax.all_gather(normed_two, "tensor", axis=0, tiled=True)
    up_values = (
        jnp.einsum("sbd,df->sbf", normed_all_two, up_full, preferred_element_type=jnp.float32)
        + up_row
    )
    activated = gelu_exact(up_values).astype(jnp.bfloat16)
    row_block = activated
    mlp_out = lax.psum_scatter(
        jnp.einsum("sbf,fd->sbd", row_block, down_full, preferred_element_type=jnp.float32),
        "tensor",
        scatter_dimension=0,
        tiled=True,
    )
    block_output = (after_attn + mlp_out + down_shift) * kept_float
    qkv_back, out_back, up_back, down_back = (qkv_matrix, out_full, up_full, down_full)
    out_grad = cotangent * kept_float
    down_shift_grad = jnp.sum(out_grad, axis=(0, 1))
    out_low = out_grad.astype(jnp.bfloat16)
    out_low_all = lax.all_gather(out_low, "tensor", axis=0, tiled=True)
    down_weight_grad = jnp.einsum(
        "sbf,sbd->fd", activated, out_low_all, preferred_element_type=jnp.float32
    )
    act_grad = jnp.einsum("sbd,fd->sbf", out_low_all, down_back, preferred_element_type=jnp.float32)
    _, gelu_back = jax.vjp(gelu_exact, up_values)
    up_grad = gelu_back(act_grad)[0].astype(jnp.bfloat16)
    up_shift_grad = jnp.sum(up_grad.astype(jnp.float32), axis=(0, 1))
    up_weight_grad = jnp.einsum(
        "sbd,sbf->df", normed_all_two, up_grad, preferred_element_type=jnp.float32
    )
    row_block = up_grad
    normed_two_grad = lax.psum_scatter(
        jnp.einsum("sbf,df->sbd", row_block, up_back, preferred_element_type=jnp.float32),
        "tensor",
        scatter_dimension=0,
        tiled=True,
    )
    _, norm_two_back = jax.vjp(layer_norm, after_attn, gain_two, shift_two)
    attn_side, gain_two_grad, shift_two_grad = norm_two_back(normed_two_grad)
    after_attn_grad = out_grad + attn_side
    out_shift_grad = jnp.sum(after_attn_grad, axis=(0, 1))
    proj_low = after_attn_grad.astype(jnp.bfloat16)
    proj_low_all = lax.all_gather(proj_low, "tensor", axis=0, tiled=True)
    out_weight_grad = jnp.einsum(
        "sbc,sbd->cd", attended_rows, proj_low_all, preferred_element_type=jnp.float32
    )
    attended_grad = jnp.einsum(
        "sbd,cd->sbc", proj_low_all, out_back, preferred_element_type=jnp.float32
    )
    attended_grad = attended_grad.astype(jnp.bfloat16)
    attended_grad_img = jnp.swapaxes(attended_grad, 0, 1).reshape(
        image_count, seq_length, head_count, HD
    )
    qkv_grad_img = lax.map(
        backward_image, (query_all, key_all, value_all, kept_all, log_totals, attended_grad_img)
    )
    qkv_grad = jnp.swapaxes(qkv_grad_img, 0, 1)
    qkv_sums = jnp.sum(qkv_grad.astype(jnp.float32), axis=(0, 1))
    qv_grad = jnp.stack([qkv_sums[:local_width], qkv_sums[2 * local_width :]], axis=0).reshape(
        2, 1, local_width
    )
    qkv_weight_grad = jnp.einsum(
        "sbd,sbc->dc", normed_all, qkv_grad, preferred_element_type=jnp.float32
    )
    qkv_weight_grad = qkv_weight_grad.reshape(model_width, 3, local_width)
    row_block = qkv_grad
    normed_one_grad = lax.psum_scatter(
        jnp.einsum("sbc,dc->sbd", row_block, qkv_back, preferred_element_type=jnp.float32),
        "tensor",
        scatter_dimension=0,
        tiled=True,
    )
    _, norm_one_back = jax.vjp(layer_norm, input_float, gain_one, shift_one)
    input_side, gain_one_grad, shift_one_grad = norm_one_back(normed_one_grad)
    input_grad = after_attn_grad + input_side
    vector_grads = jnp.stack(
        [
            gain_one_grad,
            shift_one_grad,
            out_shift_grad,
            gain_two_grad,
            shift_two_grad,
            down_shift_grad,
        ],
        axis=0,
    ).reshape(6, tensor_count, model_width // tensor_count)
    vector_local = lax.psum_scatter(vector_grads, "tensor", scatter_dimension=1, tiled=True)
    owned = (
        lax.psum_scatter(qkv_weight_grad, "dp", scatter_dimension=0, tiled=True),
        lax.psum_scatter(out_weight_grad, "dp", scatter_dimension=1, tiled=True),
        lax.psum_scatter(up_weight_grad, "dp", scatter_dimension=0, tiled=True),
        lax.psum_scatter(down_weight_grad, "dp", scatter_dimension=1, tiled=True),
        lax.psum_scatter(qv_grad, "dp", scatter_dimension=2, tiled=True),
        lax.psum_scatter(up_shift_grad.reshape(1, -1), "dp", scatter_dimension=1, tiled=True),
        lax.psum_scatter(vector_local, "dp", scatter_dimension=2, tiled=True),
    )
    qkv_owned, out_owned, up_owned, down_owned, qv_owned, hidden_owned, vector_owned = owned
    return (
        block_output,
        input_grad,
        vector_owned[0],
        vector_owned[1],
        qkv_owned,
        qv_owned,
        out_owned,
        vector_owned[2],
        vector_owned[3],
        vector_owned[4],
        up_owned,
        hidden_owned,
        down_owned,
        vector_owned[5],
    )


NT = (((1,), (1,)), ((), ()))
NN = (((1,), (0,)), ((), ()))


def dot_nn(a, b):
    return lax.dot_general(a, b, NN, preferred_element_type=F32)


def dot_nt(a, b):
    return lax.dot_general(a, b, NT, preferred_element_type=F32)


def where_key(length, values, filler):
    rest = values[SURE:]
    slot = lax.broadcasted_iota(jnp.int32, rest.shape, 0) + SURE
    return jnp.concatenate([values[:SURE], jnp.where(slot < length, rest, filler)], axis=0)


def attention_forward_kernel(lengths, q_ref, k_ref, v_ref, o_ref, lse_ref, *, key_rows):
    length = lengths[pl.program_id(0)]
    queries = q_ref[0] * jnp.asarray(HD**-0.5, BF16)
    keys = k_ref[0, :key_rows]
    values_t = jnp.transpose(v_ref[0, :key_rows].astype(F32)).astype(BF16)
    lane = lax.broadcasted_iota(jnp.int32, (key_rows, PAIR), 1)
    outs = []
    for head in range(2):
        own = (lane >= head * HD) & (lane < (head + 1) * HD)
        scores = dot_nt(jnp.where(own, keys, jnp.zeros_like(keys)), queries)
        scores = where_key(length, scores, masked_score)
        top = jnp.max(scores, axis=0, keepdims=True)
        exps = jnp.exp(scores - top)
        total = jnp.sum(exps, axis=0, keepdims=True)
        lse_ref[0, 0, head : head + 1, :] = top + jnp.log(total)
        probs = (exps * (1.0 / total)).astype(BF16)
        outs.append(dot_nn(values_t[head * HD : (head + 1) * HD], probs))
    o_ref[0] = jnp.transpose(jnp.concatenate(outs, axis=0)).astype(BF16)


def attention_backward_kernel(
    lengths, q_ref, k_ref, v_ref, lse_ref, g_ref, d_ref, *, key_rows
):
    length = lengths[pl.program_id(0)]
    slots = q_ref.shape[1]
    scale = HD**-0.5
    plain = q_ref[0]
    queries = plain * jnp.asarray(scale, BF16)
    keys = k_ref[0, :key_rows]
    values = v_ref[0, :key_rows]
    grads = g_ref[0]
    keys_t = jnp.transpose(keys.astype(F32)).astype(BF16)
    lane = lax.broadcasted_iota(jnp.int32, (key_rows, PAIR), 1)
    zero = jnp.zeros_like(keys)
    dqs, dks, dvs = [], [], []
    for head in range(2):
        own = (lane >= head * HD) & (lane < (head + 1) * HD)
        scores = dot_nt(jnp.where(own, keys, zero), queries)
        soft = where_key(length, jnp.exp(scores - lse_ref[0, 0, head : head + 1, :]), 0.0)
        prob_grad = dot_nt(jnp.where(own, values, zero), grads)
        inner = jnp.sum(prob_grad * soft, axis=0, keepdims=True)
        score_grad = (soft * (prob_grad - inner)).astype(BF16)
        dvs.append(dot_nn(soft.astype(BF16), grads))
        dks.append(dot_nn(score_grad, plain))
        dqs.append(dot_nn(keys_t[head * HD : (head + 1) * HD], score_grad))
    first = lane < HD
    d_ref[0, :, :PAIR] = (jnp.transpose(jnp.concatenate(dqs, axis=0)) * scale).astype(BF16)
    d_ref[0, :key_rows, PAIR : 2 * PAIR] = (jnp.where(first, dks[0], dks[1]) * scale).astype(BF16)
    d_ref[0, :key_rows, 2 * PAIR :] = jnp.where(first, dvs[0], dvs[1]).astype(BF16)
    if key_rows < slots:
        d_ref[0, key_rows:, PAIR:] = jnp.zeros((slots - key_rows, 2 * PAIR), BF16)


def key_count(slots):
    return min(slots, -(-VALID // 16) * 16)


def pair_block(slots, each, offset):
    return pl.BlockSpec((1, slots, PAIR), lambda b, p, ln: (b, 0, each * p + offset))


def attention_forward(lengths, qkv):
    images, slots, columns = qkv.shape
    width = columns // 3
    pairs = width // PAIR
    return pl.pallas_call(
        functools.partial(attention_forward_kernel, key_rows=key_count(slots)),
        out_shape=(
            jax.ShapeDtypeStruct((images, slots, width), BF16),
            jax.ShapeDtypeStruct((images, pairs, 2, slots), F32),
        ),
        grid_spec=pltpu.PrefetchScalarGridSpec(
            num_scalar_prefetch=1,
            grid=(images, pairs),
            in_specs=[pair_block(slots, 3, n) for n in range(3)],
            out_specs=(
                pair_block(slots, 1, 0),
                pl.BlockSpec((1, 1, 2, slots), lambda b, p, ln: (b, p, 0, 0)),
            ),
        ),
        compiler_params=pltpu.CompilerParams(vmem_limit_bytes=40 << 20),
        cost_estimate=pl.CostEstimate(
            flops=images * pairs * 2 * 4 * slots * slots * PAIR,
            bytes_accessed=images * slots * width * 8,
            transcendentals=images * pairs * 2 * slots * slots,
        ),
        name="attention_forward",
    )(lengths, qkv, qkv, qkv)


def attention_backward(lengths, qkv, lse, grads):
    images, slots, columns = qkv.shape
    width = columns // 3
    pairs = width // PAIR
    return pl.pallas_call(
        functools.partial(attention_backward_kernel, key_rows=key_count(slots)),
        out_shape=jax.ShapeDtypeStruct(qkv.shape, BF16),
        grid_spec=pltpu.PrefetchScalarGridSpec(
            num_scalar_prefetch=1,
            grid=(images, pairs),
            in_specs=[pair_block(slots, 3, n) for n in range(3)]
            + [
                pl.BlockSpec((1, 1, 2, slots), lambda b, p, ln: (b, p, 0, 0)),
                pair_block(slots, 1, 0),
            ],
            out_specs=pl.BlockSpec((1, slots, 3 * PAIR), lambda b, p, ln: (b, 0, p)),
        ),
        compiler_params=pltpu.CompilerParams(vmem_limit_bytes=40 << 20),
        cost_estimate=pl.CostEstimate(
            flops=images * pairs * 2 * 10 * slots * slots * PAIR,
            bytes_accessed=images * slots * width * 14,
            transcendentals=images * pairs * 2 * slots * slots,
        ),
        name="attention_backward",
    )(lengths, qkv, qkv, qkv, lse, grads)


def swap(array, axis, step):
    return lax.ppermute(array, axis, [(n, n ^ step) for n in range(lax.axis_size(axis))])


def shift(array, groups, by):
    count = 4 * groups
    return lax.ppermute(array, "dp", [(n, (n + 4 * by) % count) for n in range(count)])


def place():
    index = lax.axis_index("dp")
    return jnp.stack(
        [lax.axis_index("tensor"), index // 4, (index // 2) % 2, index % 2]
    ).astype(jnp.int32)


def assemble_kernel(where, *refs, groups, columns):
    *sources, out_ref, extra_ref, sems = refs
    t, z, x, c = [where[n] for n in range(4)]
    half = sources[0].shape[2]
    tail = extra_ref.shape[4]
    copies = []

    def move(source, target):
        copies.append(pltpu.make_async_copy(source, target, sems.at[len(copies)]))
        copies[-1].start()

    for turn in range(2):
        for kind in range(4):
            source = sources[4 * turn + kind]
            for near in range(2):
                for ahead in range(groups):
                    far = kind % 2
                    along_t, along_x = (far, near) if kind < 2 else (near, far)
                    rows = pl.ds((kind // 2) * half, half)
                    origin = lax.rem(z + groups - ahead, groups), x ^ along_x, c ^ turn
                    side = t ^ along_t
                    start = pl.multiple_of(side * columns, 128)
                    move(
                        source.at[near, ahead, :, pl.ds(0, columns)],
                        out_ref.at[(*origin, rows, pl.ds(start, columns))],
                    )
                    if kind < 2:
                        move(
                            source.at[near, ahead, pl.ds(0, tail), pl.ds(columns, 128)],
                            extra_ref.at[(side, *origin)],
                        )
    for copy in copies:
        copy.wait()


def gather_staged(shard, vector, coords, beside_first, after):
    rows, columns = shard.shape
    groups = lax.axis_size("dp") // 4
    entries = vector.shape[0]
    tail = 16
    beside = jnp.zeros((rows * 128,), BF16).at[:entries].set(vector).reshape(rows, 128)
    shard = jnp.concatenate([shard, beside], axis=1)
    line = jnp.stack([shard] + [shift(shard, groups, by) for by in range(1, groups)])
    line, beside_first, after = lax.optimization_barrier((line, beside_first, after))
    upper, lower = line[:, : rows // 2], line[:, rows // 2 :]
    upper = jnp.stack([upper, swap(upper, "dp", 2)])
    lower = jnp.stack([lower, swap(lower, "tensor", 1)])
    mine = [upper, swap(upper, "tensor", 1), lower, swap(lower, "dp", 2)]
    theirs = [swap(piece, "dp", 1) for piece in mine]
    anywhere = pl.BlockSpec(memory_space=pl.ANY)
    inside = pl.BlockSpec(memory_space=pltpu.VMEM)
    whole, extra = pl.pallas_call(
        functools.partial(assemble_kernel, groups=groups, columns=columns),
        out_shape=(
            jax.ShapeDtypeStruct((groups, 2, 2, rows, 2 * columns), BF16),
            jax.ShapeDtypeStruct((2, groups, 2, 2, tail, 128), BF16),
        ),
        grid_spec=pltpu.PrefetchScalarGridSpec(
            num_scalar_prefetch=1,
            in_specs=[anywhere] * 8,
            out_specs=(inside, inside),
            scratch_shapes=[pltpu.SemaphoreType.DMA((24 * groups,))],
        ),
        compiler_params=pltpu.CompilerParams(vmem_limit_bytes=(4 << 20) + 16 * groups * rows * columns),
        cost_estimate=pl.CostEstimate(
            flops=0, transcendentals=0, bytes_accessed=32 * groups * rows * columns
        ),
        name="assemble",
    )(coords, *mine, *theirs)
    extra = extra.reshape(2, 4 * groups, tail * 128)[:, :, :entries]
    return whole.reshape(4 * groups * rows, 2 * columns), extra, beside_first, after


def beside_kernel(source, out_ref):
    out_ref[...] = source[0]


def beside(gathered, offset, columns):
    rows = gathered.shape[1]
    wide = min(columns, 512)
    return pl.pallas_call(
        beside_kernel,
        out_shape=jax.ShapeDtypeStruct((rows, 2 * columns), BF16),
        grid=(2, columns // wide),
        in_specs=[pl.BlockSpec((1, rows, wide), lambda t, n: (t, 0, offset // wide + n))],
        out_specs=pl.BlockSpec((rows, wide), lambda t, n: (0, t * (columns // wide) + n)),
        compiler_params=pltpu.CompilerParams(vmem_limit_bytes=(4 << 20) + 8 * rows * wide),
        cost_estimate=pl.CostEstimate(flops=0, transcendentals=0, bytes_accessed=8 * rows * columns),
        name="beside",
    )(gathered)


def take(array, index, axis):
    return lax.dynamic_index_in_dim(array, index, axis, keepdims=False)


def side(array, index):
    half = array.shape[-1] // 2
    return lax.dynamic_slice_in_dim(array, index * half, half, array.ndim - 1)


class Sum:
    def __init__(self, whole, coords, sent=BF16):
        self.t, self.z, self.x, self.c = [coords[n] for n in range(4)]
        self.groups = lax.axis_size("dp") // 4
        self.rows = whole.shape[0] // (4 * self.groups)
        self.sent = sent
        self.state = [whole.reshape(self.groups, 2, 2, self.rows, whole.shape[1])]
        self.stage = 0

    def over_tensor(self, array):
        came = swap(side(array, 1 - self.t).astype(self.sent), "tensor", 1).astype(F32)
        return (side(array, self.t).astype(F32) + came).astype(self.sent)

    def over_pair(self, array, mine, dim, step):
        came = swap(take(array, 1 - mine, dim).astype(self.sent), "dp", step).astype(F32)
        return (take(array, mine, dim).astype(F32) + came).astype(self.sent)

    def step(self):
        half = self.rows // 2
        if self.stage == 0:
            self.state = [self.over_pair(self.state[0], self.c, 2, 1)]
        elif self.stage == 1:
            whole = self.state[0]
            self.state = [
                self.over_tensor(whole[:, :, :half]),
                self.over_pair(whole[:, :, half:], self.x, 1, 2),
            ]
        elif self.stage == 2:
            upper, lower = self.state
            self.state = [self.over_pair(upper, self.x, 1, 2), self.over_tensor(lower)]
        elif self.stage == 3:
            line = jnp.concatenate(self.state, axis=1)
            total = take(line, self.z, 0).astype(F32)
            for by in range(1, self.groups):
                sent = take(line, lax.rem(self.z + by, self.groups), 0).astype(self.sent)
                total = total + shift(sent, self.groups, by).astype(F32)
            self.state = [total]
        self.stage += 1

    def result(self):
        while self.stage < 4:
            self.step()
        return self.state[0]


def advance(sums, *values):
    for one in sums:
        one.step()
    states = [one.state for one in sums]
    values, states = lax.optimization_barrier((values, states))
    for one, state in zip(sums, states):
        one.state = state
    return values if len(values) > 1 else values[0]


def to_images(rows, after=()):
    me = lax.axis_index("tensor")
    own, part = rows.shape[0] // 2, rows.shape[1]
    kept = lax.dynamic_slice_in_dim(rows, me * own, own, 0)
    sent = lax.dynamic_slice_in_dim(rows, (1 - me) * own, own, 0)
    sent, after = lax.optimization_barrier((sent, after))
    came = lax.ppermute(sent, "tensor", [(0, 1), (1, 0)])
    whole = jnp.zeros((own, 2 * part) + rows.shape[2:], rows.dtype)
    whole = lax.dynamic_update_slice_in_dim(whole, kept, me * part, 1)
    return lax.dynamic_update_slice_in_dim(whole, came, (1 - me) * part, 1), after


def split_slots(rows, slots):
    me = lax.axis_index("tensor")
    part = slots // 2
    rows = jnp.pad(rows, ((0, 0), (0, slots - rows.shape[1]), (0, 0)))
    kept = lax.dynamic_slice_in_dim(rows, me * part, part, 1)
    sent = lax.dynamic_slice_in_dim(rows, (1 - me) * part, part, 1).astype(BF16)
    return kept, sent[:, : part // 2], sent[:, part // 2 :]


def join_slots(kept, *came):
    me = lax.axis_index("tensor")
    came = jnp.concatenate(came, axis=1).astype(kept.dtype)
    first = jnp.where(me == 0, kept, came)
    second = jnp.where(me == 0, came, kept)
    return jnp.swapaxes(jnp.concatenate([first, second], axis=0), 0, 1)


def normalize(values):
    row_mean = jnp.mean(values, axis=-1, keepdims=True)
    centred = values - row_mean
    spread = jnp.mean(centred * centred, axis=-1, keepdims=True)
    inverse = lax.rsqrt(spread + epsilon)
    return centred * inverse, inverse


def normalize_back(grad, unit, inverse, gain):
    scaled = grad * gain
    mean_one = jnp.mean(scaled, axis=-1, keepdims=True)
    mean_two = jnp.mean(scaled * unit, axis=-1, keepdims=True)
    return inverse * (scaled - mean_one - unit * mean_two)


def gelu_pair(values):
    area = 0.5 * (1.0 + lax.erf(values * (0.5**0.5)))
    density = jnp.exp(-0.5 * values * values) * ((2.0 * jnp.pi) ** -0.5)
    return (values * area).astype(BF16), area + values * density


def token_sum(values):
    return jnp.sum(values.astype(F32), axis=(0, 1))


def by_images(
    inputs,
    pad_mask,
    norm1_gain,
    norm1_shift,
    qkv_weight,
    qv_bias,
    out_weight,
    out_bias,
    norm2_gain,
    norm2_shift,
    up_weight,
    up_bias,
    down_weight,
    down_bias,
    cotangent,
):
    width = inputs.shape[2]
    slots = pad_mask.shape[1]
    used = key_count(slots)
    me = lax.axis_index("tensor")
    images = inputs.shape[1] // 2
    head_width = qkv_weight.shape[2]
    pairs = head_width // PAIR
    hidden = up_weight.shape[1]
    piece = norm1_gain.shape[1]
    depth = qkv_weight.shape[0]
    coords = place()
    product = functools.partial(jnp.einsum, preferred_element_type=F32)

    x, (qkv_weight,) = to_images(jnp.swapaxes(inputs, 0, 1), (qkv_weight,))
    vector = jnp.concatenate(
        [
            v.reshape(-1)
            for v in (norm1_gain, norm1_shift, out_bias, norm2_gain, norm2_shift, down_bias, qv_bias, up_bias)
        ]
    )
    paired = jnp.swapaxes(qkv_weight.reshape(depth, 3, pairs, PAIR), 1, 2).reshape(depth, -1)
    qkv_full, flat, x, (out_weight, up_weight, down_weight) = gather_staged(
        paired, vector, coords, x, (out_weight, up_weight, down_weight)
    )
    x = x[:, :used].astype(F32)
    flat = flat.astype(F32)
    gain_one, shift_one, out_shift, gain_two, shift_two, down_shift = [
        flat[:, :, n * piece : (n + 1) * piece].reshape(width) for n in range(6)
    ]
    query_bias = flat[:, :, 6 * piece : 7 * piece].reshape(2 * pairs, PAIR)
    value_bias = flat[:, :, 7 * piece : 8 * piece].reshape(2 * pairs, PAIR)
    qkv_bias = jnp.stack([query_bias, jnp.zeros_like(query_bias), value_bias], axis=1).reshape(-1)
    up_row = flat[:, :, 8 * piece :].reshape(2 * hidden)

    others = jnp.concatenate([jnp.transpose(out_weight), up_weight], axis=1)
    others = lax.all_gather(others, ("tensor", "dp"), axis=0, tiled=True).reshape(2, width, -1)
    out_full = beside(others, 0, head_width)
    up_full = beside(others, head_width, hidden)
    last = lax.all_gather(jnp.transpose(down_weight), ("tensor", "dp"), axis=0, tiled=True)

    here = lax.dynamic_slice_in_dim(pad_mask, me * inputs.shape[0], inputs.shape[0], 1) > 0
    down_shift_grad = token_sum(cotangent * jnp.transpose(here).astype(F32)[:, :, None])
    mask = lax.dynamic_slice_in_dim(pad_mask, me * images, images, 0)
    lengths = jnp.sum(mask, axis=1).astype(jnp.int32)
    kept = (mask[:, :used] > 0).astype(F32)[:, :, None]

    unit_one, inverse_one = normalize(x)
    normed_one = (unit_one * gain_one + shift_one).astype(BF16)
    qkv = (product("bsd,dc->bsc", normed_one, qkv_full) + qkv_bias).astype(BF16)
    cotangent, qkv = lax.optimization_barrier((cotangent, qkv))
    cot = to_images(jnp.swapaxes(cotangent.astype(BF16), 0, 1))[0][:, :used].astype(F32)
    attended, lse = attention_forward(lengths, qkv)
    projected = product("bsc,dc->bsd", attended, out_full)
    after_attn = x + projected + out_shift
    unit_two, inverse_two = normalize(after_attn)
    normed_two = (unit_two * gain_two + shift_two).astype(BF16)
    up_values = product("bsd,df->bsf", normed_two, up_full) + up_row
    act, slope = gelu_pair(up_values)
    out_low = (cot * kept).astype(BF16)
    out_grad = out_low.astype(F32)

    down = Sum(product("bsd,bsf->df", out_low, act), coords)
    out_low, last, down.state = lax.optimization_barrier((out_low, last, down.state))
    down_full = beside(last.reshape(2, width, -1), 0, hidden)
    act_grad = product("bsd,df->bsf", out_low, down_full)
    up_grad = (act_grad * slope).astype(BF16)
    up = Sum(product("bsd,bsf->df", normed_two, up_grad), coords)
    up_shift_grad = token_sum(up_grad)
    down.step()
    up_grad, down.state, up.state = lax.optimization_barrier((up_grad, down.state, up.state))
    normed_two_grad = product("bsf,df->bsd", up_grad, up_full)
    normed_two_grad = advance([down, up], normed_two_grad)
    gain_two_grad = token_sum(normed_two_grad * unit_two)
    shift_two_grad = token_sum(normed_two_grad)
    after_attn_grad = out_grad + normalize_back(normed_two_grad, unit_two, inverse_two, gain_two)
    out_shift_grad = token_sum(after_attn_grad)
    proj_low = after_attn_grad.astype(BF16)
    out = Sum(product("bsd,bsc->dc", proj_low, attended), coords)
    attended_grad = product("bsd,dc->bsc", proj_low, out_full).astype(BF16)
    attended_grad, act = advance([down], attended_grad, act)
    mlp_out = product("bsf,df->bsd", act, down_full)
    finished = (after_attn + mlp_out + down_shift) * kept
    down.step()
    up.step()
    attended_grad, qkv, finished, out.state, down.state, up.state = lax.optimization_barrier(
        (attended_grad, qkv, finished, out.state, down.state, up.state)
    )
    qkv_grad = attention_backward(lengths, qkv, lse, attended_grad)
    held, near, far = split_slots(finished, slots)
    block_output = join_slots(held, swap(near, "tensor", 1), swap(far, "tensor", 1))
    qkv_grad, normed_one, block_output = advance([up, out], qkv_grad, normed_one, block_output)
    qkv_sum = Sum(product("bsd,bsc->dc", normed_one, qkv_grad), coords)
    qkv_grad = advance([up, out], qkv_grad)
    normed_one_grad = product("bsc,dc->bsd", qkv_grad, qkv_full)
    bias_sums = token_sum(qkv_grad).reshape(2 * pairs, 3, PAIR)
    normed_one_grad = advance([out, qkv_sum], normed_one_grad)
    gain_one_grad = token_sum(normed_one_grad * unit_one)
    shift_one_grad = token_sum(normed_one_grad)
    input_grad = after_attn_grad + normalize_back(normed_one_grad, unit_one, inverse_one, gain_one)
    input_grad, gain_one_grad, shift_one_grad = advance(
        [out, qkv_sum], input_grad, gain_one_grad, shift_one_grad
    )

    vectors = [gain_one_grad, shift_one_grad, out_shift_grad, gain_two_grad, shift_two_grad, down_shift_grad]
    vectors += [bias_sums[:, 0], bias_sums[:, 2], up_shift_grad]
    small = jnp.concatenate([v.reshape(2, lax.axis_size("dp"), -1) for v in vectors], axis=2)
    entries = small.shape[2]
    small = jnp.swapaxes(small.reshape(2, -1, entries // 2), 0, 1).reshape(-1, entries)
    small = Sum(small, coords, F32)
    held, near, far = split_slots(input_grad, slots)
    near_came = swap(near, "tensor", 1)
    near_came, far = advance([small, qkv_sum], near_came, far)
    far_came = swap(far, "tensor", 1)
    far_came, near_came = advance([small, qkv_sum], far_came, near_came)
    input_grad = join_slots(held, near_came, far_came)
    total = qkv_sum.result()
    small = small.result().reshape(1, entries)
    row = lambda n: small[:, n * piece : (n + 1) * piece]
    qkv_owned = jnp.swapaxes(total.reshape(depth, pairs, 3, PAIR), 1, 2)
    return (
        block_output,
        input_grad,
        row(0),
        row(1),
        qkv_owned.reshape(qkv_weight.shape),
        jnp.stack([row(6), row(7)], axis=0),
        jnp.transpose(out.result()),
        row(2),
        row(3),
        row(4),
        up.result(),
        small[:, 8 * piece :],
        jnp.transpose(down.result()),
        row(5),
    )


def solution(mesh):
    in_specs = (
        P("tensor", "dp", None),
        P("dp", None),
        P("tensor", "dp"),
        P("tensor", "dp"),
        P("dp", None, "tensor"),
        P(None, "tensor", "dp"),
        P("tensor", "dp"),
        P("tensor", "dp"),
        P("tensor", "dp"),
        P("tensor", "dp"),
        P("dp", "tensor"),
        P("tensor", "dp"),
        P("tensor", "dp"),
        P("tensor", "dp"),
        P("tensor", "dp", None),
    )
    out_specs = (
        P("tensor", "dp", None),
        P("tensor", "dp", None),
        P("tensor", "dp"),
        P("tensor", "dp"),
        P("dp", None, "tensor"),
        P(None, "tensor", "dp"),
        P("tensor", "dp"),
        P("tensor", "dp"),
        P("tensor", "dp"),
        P("tensor", "dp"),
        P("dp", "tensor"),
        P("tensor", "dp"),
        P("tensor", "dp"),
        P("tensor", "dp"),
    )
    dims = dict(zip(mesh.axis_names, mesh.devices.shape))

    def choose(inputs, *rest):
        whole_images = dims["tensor"] == 2 and dims["dp"] % 4 == 0 and inputs.shape[1] % 2 == 0
        return (by_images if whole_images else on_device)(inputs, *rest)

    return jax.shard_map(
        choose, mesh=mesh, in_specs=in_specs, out_specs=out_specs, check_vma=False
    )
```
